32 devices in a mesh: tensor: 4 (over z), dp: 4 (over y, x), seq: 2 (over core).
Axes of the slice: x: 2, y: 2, z: 4, core: 2. Of those that a mesh axis runs over, the one named last changes fastest.
Arguments:
- block_input: bfloat16 [4, 768, 1024], P('dp', 'seq'), may hold values from -6 to 6
- mixer_gain: float32 [1024], replicated, may hold values from 0.5 to 1.5
- query_weight: bfloat16 [1024, 512], P(None, 'tensor'), may hold values from -0.1875 to 0.1875
- key_weight: bfloat16 [1024, 512], P(None, 'tensor'), may hold values from -0.1875 to 0.1875
- value_weight: bfloat16 [1024, 1024], P(None, 'tensor'), may hold values from -0.1875 to 0.1875
- outgate_weight: bfloat16 [1024, 1024], P(None, 'tensor'), may hold values from -0.1875 to 0.1875
- decay_down: bfloat16 [1024, 16], replicated, may hold values from -0.1875 to 0.1875
- decay_up: bfloat16 [16, 512], P(None, 'tensor'), may hold values from -1.5 to 1.5
- decay_bias: float32 [512], P('tensor'), may hold values from -1 to 6
- group_gain: float32 [256], replicated, may hold values from 0.5 to 1.5
- output_weight: bfloat16 [1024, 1024], P('tensor'), may hold values from -0.25 to 0.25
- swiglu_gain: float32 [1024], replicated, may hold values from 0.5 to 1.5
- gate_weight: bfloat16 [1024, 2816], P(None, 'tensor'), may hold values from -0.1875 to 0.1875
- up_weight: bfloat16 [1024, 2816], P(None, 'tensor'), may hold values from -0.1875 to 0.1875
- down_weight: bfloat16 [2816, 1024], P('tensor'), may hold values from -0.15625 to 0.15625
- cotangent: bfloat16 [4, 768, 1024], P('dp', 'seq'), may hold values from -6 to 6
Outputs:
- block_output: bfloat16 [4, 768, 1024], P('dp', 'seq')
- input_gradient: float32 [4, 768, 1024], P('dp', 'seq', 'tensor')
- mixer_gradient: float32 [1024], P('tensor')
- query_gradient: float32 [1024, 512], P(('dp', 'seq'), 'tensor')
- key_gradient: float32 [1024, 512], P(('dp', 'seq'), 'tensor')
- value_gradient: float32 [1024, 1024], P(('dp', 'seq'), 'tensor')
- outgate_gradient: float32 [1024, 1024], P(('dp', 'seq'), 'tensor')
- lowrank_gradient: float32 [1024, 16], replicated
- decay_gradient: float32 [16, 512], P(None, 'tensor')
- bias_gradient: float32 [512], P('tensor')
- group_gradient: float32 [256], replicated
- output_gradient: float32 [1024, 1024], P('tensor', ('dp', 'seq'))
- swiglu_gradient: float32 [1024], replicated
- gate_gradient: float32 [1024, 2816], P(('dp', 'seq'), 'tensor')
- up_gradient: float32 [1024, 2816], P(('dp', 'seq'), 'tensor')
- down_gradient: float32 [2816, 1024], P('tensor', ('dp', 'seq'))
The draws below stay inside these ranges and needn't reach their ends.
All inputs are finite; a program needn't handle non-finite values.
Results may differ from the reference program's by a relative error of at most 0.011.
Values sent between devices are 32-bit elements; how exact they have to be, the bound alone decides.
No kernel may reach another device: no remote copies, remote signals or barrier semaphores. Data moves between devices by JAX's collectives and lax.ppermute only.
A program may use at most 192 MiB of HBM per device.

```python
import jax
import jax.numpy as jnp
from jax import lax

D = 1024
HEADS = 4
DK = 128
DV = 256
RANK = 16
FF = 2816
SPAN = 64
SEQS = 4
LEN = 768


def with_spikes(result, key, source, target, blocks, factor):
    owner, partner = [(jnp.arange(result.shape[dim]) // (result.shape[dim] // blocks)).reshape([-1 if axis == dim else 1 for axis in range(result.ndim)]) for dim in (source, target)]
    chosen = jax.random.permutation(key, blocks)[partner]
    strong = (owner == chosen) | (owner == (partner + blocks // 2) % blocks)
    return jnp.where(strong, factor * result, result)


def block_scale(key, dims, split, low, high):
    level, own = 1.0, jax.random.fold_in(key, 6)
    for position, blocks in split:
        draws = jnp.exp(jax.random.uniform(jax.random.fold_in(own, position), (blocks,), jnp.float32, low / len(split), high / len(split)))
        level = level * jnp.repeat(draws, dims[position] // blocks).reshape([-1 if axis == position else 1 for axis in range(len(dims))])
    return level


def gaussian(key, dims, scale, reach, cuts=(), kind=jnp.bfloat16):
    entries = jax.random.normal(key, dims, jnp.float32) * scale
    if len(cuts) > 0:
        entries = block_scale(key, dims, cuts, -0.22, 0.18) * entries
    return jnp.clip(entries, min=-reach, max=reach).astype(kind)


def bell_draw_with(rng, shape, scale, reach, cuts, heavy, held_as=jnp.bfloat16):
    result = scale * jax.random.normal(rng, shape, jnp.float32)
    if cuts:
        result = result * block_scale(rng, shape, cuts, -0.22, 0.18)
    return jnp.clip(with_spikes(result, jax.random.fold_in(rng, 3), *heavy), -reach, reach).astype(held_as)


def setup_inputs(seed: int = 0) -> dict:
    arg_keys = jax.random.split(jax.random.key(seed), 17)
    block_input = bell_draw_with(arg_keys[0], (SEQS, LEN, D), 1.0, 6.0, ((0, 4), (1, 2)), (0, 2, 4, 2.0))
    mixer_gain = jnp.clip(1.0 + 0.1 * jax.random.normal(arg_keys[1], (D,), jnp.float32), 0.5, 1.5)
    query_weight = gaussian(arg_keys[2], (D, HEADS * DK), D ** -0.5, 0.1875, ((1, 4),))
    key_weight = gaussian(arg_keys[3], (D, HEADS * DK), D ** -0.5, 0.1875, ((1, 4),))
    value_weight = gaussian(arg_keys[4], (D, HEADS * DV), D ** -0.5, 0.1875, ((1, 4),))
    outgate_weight = gaussian(arg_keys[5], (D, HEADS * DV), D ** -0.5, 0.1875, ((1, 4),))
    decay_down = gaussian(arg_keys[6], (D, RANK), D ** -0.5, 0.1875)
    decay_up = gaussian(arg_keys[7], (RANK, HEADS * DK), RANK ** -0.5, 1.5, ((1, 4),))
    decay_bias = jnp.clip(-1.0 + 7.0 * jax.random.uniform(arg_keys[8], (HEADS * DK,), jnp.float32) ** block_scale(arg_keys[8], (HEADS * DK,), ((0, 4),), -0.2, 0.2), -1.0, 6.0)
    group_gain = jnp.clip(1.0 + 0.1 * jax.random.normal(arg_keys[9], (DV,), jnp.float32), 0.5, 1.5)
    output_weight = gaussian(arg_keys[10], (HEADS * DV, D), (HEADS * DV // 2) ** -0.5, 0.25, ((0, 4),))
    swiglu_gain = jnp.clip(1.0 + 0.1 * jax.random.normal(arg_keys[11], (D,), jnp.float32), 0.5, 1.5)
    gate_weight = gaussian(arg_keys[12], (D, FF), D ** -0.5, 0.1875, ((1, 4),))
    up_weight = gaussian(arg_keys[13], (D, FF), D ** -0.5, 0.1875, ((1, 4),))
    down_weight = gaussian(arg_keys[14], (FF, D), (FF // 2) ** -0.5, 0.15625, ((0, 4),))
    cotangent = bell_draw_with(arg_keys[15], (SEQS, LEN, D), 1.0, 6.0, ((0, 4), (1, 2)), (0, 2, 4, 2.0))
    return {"block_input": block_input, "mixer_gain": mixer_gain, "query_weight": query_weight, "key_weight": key_weight, "value_weight": value_weight, "outgate_weight": outgate_weight, "decay_down": decay_down, "decay_up": decay_up, "decay_bias": decay_bias, "group_gain": group_gain, "output_weight": output_weight, "swiglu_gain": swiglu_gain, "gate_weight": gate_weight, "up_weight": up_weight, "down_weight": down_weight, "cotangent": cotangent}


EPS = 1e-06
GATE_NORM = 16.0
highest_precision = lax.Precision.HIGHEST

def product(left, right):
    return jnp.dot(left, right, preferred_element_type=jnp.float32)

def rms_apply(values, gain):
    return values * lax.rsqrt(lax.optimization_barrier(jnp.mean(values * values, axis=-1, keepdims=True)) + EPS) * gain

def gate_apply(mixed_output, group_gain, outgate):
    rows = mixed_output.shape[0]
    shaped = mixed_output.reshape(rows, -1, DV)
    normed = rms_apply(shaped, group_gain)
    return (normed * jax.nn.silu(outgate.reshape(rows, -1, DV))).reshape(rows, -1)

def forget_log(lowrank, expand, bias):
    return jax.nn.log_sigmoid(jnp.dot(lowrank, expand, precision=highest_precision) + bias) / GATE_NORM

def span_mix(query, keyrow, value, forget, running_state):
    length, heads, kdim = query.shape
    vdim = value.shape[2]
    blocks = length // SPAN
    scale = kdim ** (-0.5)
    qblock = query.reshape(blocks, SPAN, heads, kdim)
    kblock = keyrow.reshape(blocks, SPAN, heads, kdim)
    vblock = value.reshape(blocks, SPAN, heads, vdim)
    cumul = jnp.cumsum(forget.reshape(blocks, SPAN, heads, kdim), axis=1)
    lower = (jnp.arange(SPAN)[:, None] >= jnp.arange(SPAN)[None, :])[:, :, None, None]

    def advance(scan_carry, item):
        query_slice, key_slice, value_slice, cumulative_slice = item
        finalize_output = cumulative_slice[-1]
        cross_segment = jnp.einsum('eyp,ypf->eyf', query_slice * jnp.exp(cumulative_slice), scan_carry, precision=highest_precision)
        spread = cumulative_slice[:, None] - cumulative_slice[None, :]
        decay = jnp.where(lower, jnp.exp(jnp.where(lower, spread, 0.0)), 0.0)
        scores = lax.optimization_barrier(jnp.sum(query_slice[:, None] * key_slice[None, :] * decay, axis=-1))
        intra = jnp.einsum('ijh,jhv->ihv', scores, value_slice, precision=highest_precision)
        scan_carry = jnp.exp(finalize_output)[:, :, None] * scan_carry + jnp.einsum('lta,ltz->taz', key_slice * jnp.exp(finalize_output[None] - cumulative_slice), value_slice, precision=highest_precision)
        return (scan_carry, (cross_segment + intra) * scale)
    running_state, outputs = lax.scan(advance, running_state, (qblock, kblock, vblock, cumul))
    return (outputs.reshape(length, heads, vdim), running_state)

def reference(block_input, mixer_gain, query_weight, key_weight, value_weight, outgate_weight, decay_down, decay_up, decay_bias, group_gain, output_weight, swiglu_gain, gate_weight, up_weight, down_weight, cotangent):
    expand = decay_up.astype(jnp.float32)
    heads = query_weight.shape[1] // DK

    def per_sequence(totals, item):
        rows, upstream = item
        length = rows.shape[0]
        source = rows.astype(jnp.float32)
        normed_b = rms_apply(source, mixer_gain).astype(jnp.bfloat16)
        query = product(normed_b, query_weight)
        keyrow = product(normed_b, key_weight)
        value = product(normed_b, value_weight)
        outgate = product(normed_b, outgate_weight)
        lowrank = product(normed_b, decay_down)
        forget = forget_log(lowrank, expand, decay_bias)
        zero_state = jnp.zeros((heads, DK, DV), jnp.float32)
        query3 = query.reshape(length, heads, DK)
        key3 = keyrow.reshape(length, heads, DK)
        value3 = value.reshape(length, heads, DV)
        forget3 = forget.reshape(length, heads, DK)
        mixed_output3, unused = span_mix(query3, key3, value3, forget3, zero_state)
        mixed_output = mixed_output3.reshape(length, -1)
        gated_b = gate_apply(mixed_output, group_gain, outgate).astype(jnp.bfloat16)
        middle = source + product(gated_b, output_weight)
        second_b = rms_apply(middle, swiglu_gain).astype(jnp.bfloat16)
        gate_pre = product(second_b, gate_weight)
        up_pre = product(second_b, up_weight)
        hidden_b = (jax.nn.silu(gate_pre) * up_pre).astype(jnp.bfloat16)
        block_output = (middle + product(hidden_b, down_weight)).astype(jnp.bfloat16)
        hidden_back = product(upstream, down_weight.T)
        down_part = product(hidden_b.T, upstream)
        unused, swiglu_vjp = jax.vjp(lambda gvals, uvals: jax.nn.silu(gvals) * uvals, gate_pre, up_pre)
        gate_back, up_back = swiglu_vjp(hidden_back)
        gate_back_b = gate_back.astype(jnp.bfloat16)
        up_back_b = up_back.astype(jnp.bfloat16)
        gate_part = product(second_b.T, gate_back_b)
        up_part = product(second_b.T, up_back_b)
        second_back = product(gate_back_b, gate_weight.T) + product(up_back_b, up_weight.T)
        unused, norm_vjp = jax.vjp(rms_apply, middle, swiglu_gain)
        middle_back, swiglu_part = norm_vjp(second_back)
        middle_back = middle_back + upstream.astype(jnp.float32)
        middle_round = middle_back.astype(jnp.bfloat16)
        gated_back = product(middle_round, output_weight.T)
        output_part = product(gated_b.T, middle_round)
        unused, gate_vjp = jax.vjp(gate_apply, mixed_output, group_gain, outgate)
        mixed_back, group_part, outgate_back = gate_vjp(gated_back)
        unused, mix_vjp = jax.vjp(lambda qa, ka, va, fa: span_mix(qa, ka, va, fa, zero_state)[0], query3, key3, value3, forget3)
        query_back, key_back, value_back, forget_back = mix_vjp(mixed_back.reshape(length, heads, DV))
        unused, forget_vjp = jax.vjp(forget_log, lowrank, expand, decay_bias)
        lowrank_back, expand_part, bias_part = forget_vjp(forget_back.reshape(length, -1))
        query_round = query_back.reshape(length, -1).astype(jnp.bfloat16)
        key_round = key_back.reshape(length, -1).astype(jnp.bfloat16)
        value_round = value_back.reshape(length, -1).astype(jnp.bfloat16)
        outgate_round = outgate_back.astype(jnp.bfloat16)
        lowrank_round = lowrank_back.astype(jnp.bfloat16)
        normed_back = product(query_round, query_weight.T) + product(key_round, key_weight.T) + product(value_round, value_weight.T) + product(outgate_round, outgate_weight.T) + product(lowrank_round, decay_down.T)
        unused, first_vjp = jax.vjp(rms_apply, source, mixer_gain)
        source_back, mixer_part = first_vjp(normed_back)
        input_gradient = middle_back + source_back
        parts = (mixer_part, product(normed_b.T, query_round), product(normed_b.T, key_round), product(normed_b.T, value_round), product(normed_b.T, outgate_round), product(normed_b.T, lowrank_round), expand_part, bias_part, group_part, output_part, swiglu_part, gate_part, up_part, down_part)
        totals = tuple((total + part for total, part in zip(totals, parts)))
        return (totals, (block_output, input_gradient))
    starting = (jnp.zeros((D,), jnp.float32), jnp.zeros(query_weight.shape, jnp.float32), jnp.zeros(key_weight.shape, jnp.float32), jnp.zeros(value_weight.shape, jnp.float32), jnp.zeros(outgate_weight.shape, jnp.float32), jnp.zeros(decay_down.shape, jnp.float32), jnp.zeros(decay_up.shape, jnp.float32), jnp.zeros(decay_bias.shape, jnp.float32), jnp.zeros(group_gain.shape, jnp.float32), jnp.zeros(output_weight.shape, jnp.float32), jnp.zeros((D,), jnp.float32), jnp.zeros(gate_weight.shape, jnp.float32), jnp.zeros(up_weight.shape, jnp.float32), jnp.zeros(down_weight.shape, jnp.float32))
    totals, outputs = lax.scan(per_sequence, starting, (block_input, cotangent))
    return (outputs[0], outputs[1], totals[0], totals[1], totals[2], totals[3], totals[4], totals[5], totals[6], totals[7], totals[8], totals[9], totals[10], totals[11], totals[12], totals[13])
```

```python
import functools

import jax
import jax.numpy as jnp
from jax import lax
from jax.experimental import pallas as pl
from jax.experimental.pallas import tpu as pltpu
from jax.sharding import PartitionSpec as P

DK = 128
DV = 256
SPAN = 64
TILE = 8
PARTS = 2
ORDER = (0, 1, 3, 2)
VMEM_LIMIT = 32 * 2**20


EPS = 1e-06
GATE_NORM = 16.0
highest_precision = lax.Precision.HIGHEST


def flip(values, axis, mask):
    count = lax.axis_size(axis)
    return lax.ppermute(values, axis, [(i, i ^ mask) for i in range(count)])


def butterfly(values, axis, first=1):
    count = lax.axis_size(axis)
    mask = first
    while mask < count:
        values = values + flip(values, axis, mask)
        mask *= 2
    return values


def halves_sum(sent, kept):
    if lax.axis_size("tensor") == 1:
        return kept, sent
    kept = butterfly(kept + flip(sent, "tensor", 1), "tensor", 2)
    return kept, flip(kept, "tensor", 1)


def upper_half():
    return lax.axis_index("tensor") % 2


def column_block(values, block, width):
    return lax.dynamic_slice_in_dim(values, block * width, width, 1)


def direct():
    return lax.axis_size("dp") == 4 and lax.axis_size("seq") == 2


def scatter_pair(sent, kept):
    size = kept.shape[0] // 4
    cut = kept.shape[1] // 256 * 128
    near = kept + flip(sent, "seq", 1)
    one, two = near[:, :cut], near[:, cut:]
    got = flip(one[size : 3 * size], "dp", 1)
    far = flip(two[2 * size :], "dp", 2)
    one = one[:size] + got[:size] + flip(one[3 * size :] + got[size:], "dp", 2)
    two = two[:size] + far[size:] + flip(two[size : 2 * size] + far[:size], "dp", 1)
    return one, two


def product(left, right):
    return jnp.dot(left, right, preferred_element_type=jnp.float32)


def rms_apply(values, gain):
    return values * lax.rsqrt(jnp.mean(values * values, axis=-1, keepdims=True) + EPS) * gain


MIX_PRECISION = lax.Precision.HIGHEST


def contract(left, right, left_dim, right_dim, precision=MIX_PRECISION):
    return lax.dot_general(
        left,
        right,
        (((left_dim,), (right_dim,)), ((), ())),
        precision=precision,
        preferred_element_type=jnp.float32,
    )


def exact(left, right, left_dim, right_dim):
    return contract(left, right, left_dim, right_dim, highest_precision)


def grid_of(shape, dim):
    return lax.broadcasted_iota(jnp.int32, shape, dim)


def level_masks(span):
    row, col = grid_of((span, span), 0), grid_of((span, span), 1)
    masks = []
    half = span // 2
    while half >= TILE:
        masks.append((half, (row // (2 * half) == col // (2 * half)) & (row // half > col // half)))
        half //= 2
    return masks, (row // TILE == col // TILE) & (row >= col), col % TILE


def level_decay(cumul, half):
    rows, width = cumul.shape
    middle = [
        jnp.broadcast_to(cumul[start + half - 1 : start + half], (2 * half, width))
        for start in range(0, rows, 2 * half)
    ]
    return jnp.exp(-jnp.abs(cumul - jnp.concatenate(middle, axis=0)))


def tiles(values):
    return values.reshape(values.shape[0] // TILE, TILE, values.shape[1])


def span_scores(query, keyrow, cumul, masks, near, place):
    span = query.shape[0]
    scores = jnp.zeros((span, span), jnp.float32)
    for half, mask in masks:
        decay = level_decay(cumul, half)
        scores = scores + jnp.where(mask, contract(query * decay, keyrow * decay, 1, 1), 0.0)
    query3, key3, cumul3 = tiles(query), tiles(keyrow), tiles(cumul)
    close = jnp.zeros((span, span), jnp.float32)
    for step in range(TILE):
        decay = jnp.exp(jnp.minimum(cumul3 - cumul3[:, step : step + 1], 0.0))
        terms = (query3 * key3[:, step : step + 1] * decay).reshape(span, -1)
        close = jnp.where(place == step, jnp.sum(terms, axis=-1, keepdims=True), close)
    return scores + jnp.where(near, close, 0.0)


def triangle(span, upper):
    row, col = grid_of((span, span), 0), grid_of((span, span), 1)
    return jnp.where(row <= col if upper else row >= col, 1.0, 0.0).astype(jnp.float32)


def mix_forward(
    source_ref,
    gain_ref,
    query_w,
    key_w,
    value_w,
    outgate_w,
    down_w,
    up_w,
    bias_ref,
    normed_ref,
    query_ref,
    key_ref,
    value_ref,
    outgate_ref,
    lowrank_ref,
    logit_ref,
    cumul_ref,
    reach_ref,
    local_ref,
    state_ref,
    total_ref,
):
    length = source_ref.shape[0]
    heads = query_w.shape[1] // DK
    normed = rms_apply(source_ref[...].astype(jnp.float32), gain_ref[...]).astype(jnp.bfloat16)
    normed_ref[...] = normed
    lowrank = product(normed, down_w[...])
    lowrank_ref[...] = lowrank
    logit = exact(lowrank, up_w[...].astype(jnp.float32), 1, 0) + bias_ref[...]
    logit_ref[...] = logit
    forget = (jnp.minimum(logit, 0.0) - jnp.log1p(jnp.exp(-jnp.abs(logit)))) / GATE_NORM
    query_ref[...] = product(normed, query_w[...])
    key_ref[...] = product(normed, key_w[...])
    value_ref[...] = product(normed, value_w[...])
    outgate_ref[...] = product(normed, outgate_w[...])
    masks, near, place = level_masks(SPAN)
    lower = triangle(SPAN, False)
    scale = DK ** (-0.5)
    for head in range(heads):
        narrow = slice(head * DK, (head + 1) * DK)
        wide = slice(head * DV, (head + 1) * DV)
        state = None
        base = jnp.zeros((1, DK), jnp.float32)
        for start in range(0, length, SPAN):
            rows = slice(start, start + SPAN)
            query, keyrow, value = query_ref[rows, narrow], key_ref[rows, narrow], value_ref[rows, wide]
            cumul = exact(lower, forget[rows, narrow], 1, 0)
            cumul_ref[rows, narrow] = cumul
            last = cumul[SPAN - 1 : SPAN]
            reach_ref[rows, narrow] = query * jnp.exp(cumul + base) * scale
            base = base + last
            scores = span_scores(query, keyrow, cumul, masks, near, place)
            mixed = contract(scores, value, 1, 0)
            if state is not None:
                mixed = mixed + contract(query * jnp.exp(cumul), state, 1, 1)
            local_ref[rows, wide] = mixed * scale
            added = contract(value, keyrow * jnp.exp(last - cumul), 0, 0)
            state = added if state is None else state * jnp.exp(last) + added
        state_ref[wide, :] = state
        total_ref[head : head + 1, :] = jnp.exp(base)


def mix_backward(
    query_ref,
    key_ref,
    value_ref,
    cumul_ref,
    logit_ref,
    lowrank_ref,
    mixed_back_ref,
    state_ref,
    state_back_ref,
    up_w,
    query_back_ref,
    key_back_ref,
    value_back_ref,
    lowrank_back_ref,
    expand_ref,
    bias_ref,
    states_ref,
    logit_back_ref,
):
    length = query_ref.shape[0]
    heads = query_ref.shape[1] // DK
    count = length // SPAN
    masks, near, place = level_masks(SPAN)
    upper = triangle(SPAN, True)
    scale = DK ** (-0.5)
    final = grid_of((SPAN, DK), 0) == SPAN - 1
    lane_row = grid_of((SPAN // TILE, TILE, DK), 1)
    for head in range(heads):
        narrow = slice(head * DK, (head + 1) * DK)
        wide = slice(head * DV, (head + 1) * DV)
        state = state_ref[wide, :]
        for index in range(count):
            rows = slice(index * SPAN, (index + 1) * SPAN)
            states_ref[index] = state
            cumul = cumul_ref[rows, narrow]
            last = cumul[SPAN - 1 : SPAN]
            state = state * jnp.exp(last) + contract(
                value_ref[rows, wide], key_ref[rows, narrow] * jnp.exp(last - cumul), 0, 0
            )
        after = state
        carried = state_back_ref[wide, :]
        for index in reversed(range(count)):
            rows = slice(index * SPAN, (index + 1) * SPAN)
            query, keyrow, value = query_ref[rows, narrow], key_ref[rows, narrow], value_ref[rows, wide]
            cumul = cumul_ref[rows, narrow]
            last = cumul[SPAN - 1 : SPAN]
            back = mixed_back_ref[rows, wide] * scale
            before = states_ref[index]
            grown, rest = jnp.exp(cumul), jnp.exp(last - cumul)
            scores = span_scores(query, keyrow, cumul, masks, near, place)
            value_back = contract(scores, back, 0, 0) + contract(keyrow * rest, carried, 1, 1)
            value_back_ref[rows, wide] = value_back.astype(jnp.bfloat16)
            pairs = contract(back, value, 1, 1)
            query_back = grown * contract(back, before, 1, 0)
            key_back = rest * contract(value, carried, 1, 0)
            for half, mask in masks:
                decay = level_decay(cumul, half)
                chosen = jnp.where(mask, pairs, 0.0)
                query_back = query_back + decay * contract(chosen, keyrow * decay, 1, 0)
                key_back = key_back + decay * contract(chosen, query * decay, 0, 0)
            close = jnp.where(near, pairs, 0.0)
            query3, key3, cumul3 = tiles(query), tiles(keyrow), tiles(cumul)
            query_near = jnp.zeros_like(query3)
            key_near = jnp.zeros_like(key3)
            for step in range(TILE):
                column = jnp.sum(jnp.where(place == step, close, 0.0), axis=-1, keepdims=True)
                decay = jnp.exp(jnp.minimum(cumul3 - cumul3[:, step : step + 1], 0.0))
                weight = tiles(jnp.broadcast_to(column, (SPAN, DK))) * decay
                query_near = query_near + weight * key3[:, step : step + 1]
                total = jnp.sum(weight * query3, axis=1, keepdims=True)
                key_near = jnp.where(lane_row == step, total, key_near)
            query_back = query_back + query_near.reshape(SPAN, DK)
            key_back = key_back + key_near.reshape(SPAN, DK)
            query_back_ref[rows, narrow] = query_back.astype(jnp.bfloat16)
            key_back_ref[rows, narrow] = key_back.astype(jnp.bfloat16)
            cumul_back = query * query_back - keyrow * key_back
            ending = jnp.sum(after * carried, axis=0, keepdims=True)
            cumul_back = cumul_back + jnp.where(final, ending, 0.0)
            forget_back = exact(upper, cumul_back, 1, 0)
            logit_back_ref[rows, narrow] = forget_back * jax.nn.sigmoid(-logit_ref[rows, narrow]) / GATE_NORM
            carried = carried * jnp.exp(last) + contract(back, query * grown, 0, 0)
            after = before
    logit_back = logit_back_ref[...]
    lowrank_back_ref[...] = exact(logit_back, up_w[...].astype(jnp.float32), 1, 1).astype(jnp.bfloat16)
    expand_ref[...] = exact(lowrank_ref[...], logit_back, 0, 0)
    bias_ref[...] = jnp.sum(logit_back, axis=0, keepdims=True)


def call(kernel, outs, flops, scratch=(), name=None):
    whole = pl.BlockSpec(memory_space=pltpu.VMEM)

    def run(*args):
        moved = sum(a.size * a.dtype.itemsize for a in args)
        moved += sum(o.size * o.dtype.itemsize for o in outs)
        return pl.pallas_call(
            kernel,
            out_shape=tuple(outs),
            in_specs=[whole] * len(args),
            out_specs=tuple([whole] * len(outs)),
            scratch_shapes=list(scratch),
            name=name,
            compiler_params=pltpu.CompilerParams(vmem_limit_bytes=VMEM_LIMIT),
            cost_estimate=pl.CostEstimate(flops=flops, bytes_accessed=moved, transcendentals=0),
        )(*args)

    return run


def shape_of(rows, cols, kind=jnp.float32):
    return jax.ShapeDtypeStruct((rows, cols), kind)


def relay(own, total, axis, reverse):
    count = lax.axis_size(axis)
    pairs = [(i + 1, i) if reverse else (i, i + 1) for i in range(count - 1)]
    entering = None
    for _ in range(count - 1):
        sent = own if entering is None else own + total * entering
        entering = lax.ppermute(sent, axis, pairs)
    return jnp.zeros_like(own) if entering is None else entering


def split_halves(value, sent_ref, kept_ref, work_ref):
    half = value.shape[0] // 2
    work_ref[...] = value
    upper = upper_half()
    kept_ref[...] = work_ref[pl.ds(pl.multiple_of(upper * half, half), half), :]
    sent_ref[...] = work_ref[pl.ds(pl.multiple_of((1 - upper) * half, half), half), :]


def join_halves(kept_ref, other_ref, work_ref):
    half = kept_ref.shape[0]
    upper = upper_half()
    work_ref[pl.ds(pl.multiple_of(upper * half, half), half), :] = kept_ref[...]
    work_ref[pl.ds(pl.multiple_of((1 - upper) * half, half), half), :] = other_ref[...]
    return work_ref[...]


def gate_forward(local_ref, reach_ref, state_ref, outgate_ref, gain_ref, weight_ref, *rest):
    mixed_ref, gated_ref = rest[:2]
    pieces, work_ref = rest[2:-1], rest[-1]
    heads = local_ref.shape[1] // DV
    for head in range(heads):
        narrow = slice(head * DK, (head + 1) * DK)
        wide = slice(head * DV, (head + 1) * DV)
        mixed = local_ref[:, wide] + contract(reach_ref[:, narrow], state_ref[wide, :], 1, 1)
        mixed_ref[:, wide] = mixed
        gate = outgate_ref[:, wide]
        gated = rms_apply(mixed, gain_ref[...]) * (gate * jax.nn.sigmoid(gate))
        gated_ref[:, wide] = gated.astype(jnp.bfloat16)
    size = local_ref.shape[0] // PARTS
    for part in range(PARTS):
        terms = product(gated_ref[part * size : (part + 1) * size, :], weight_ref[...])
        split_halves(terms, pieces[2 * part], pieces[2 * part + 1], work_ref)


def feed_forward(
    kept_ref,
    other_ref,
    source_ref,
    upstream_ref,
    gain_ref,
    gate_w,
    up_w,
    down_w,
    middle_ref,
    second_ref,
    hidden_ref,
    back_ref,
    second_sent,
    second_kept,
    output_sent,
    output_kept,
    work_ref,
    *,
    part,
):
    size = middle_ref.shape[0]
    rows = slice(part * size, (part + 1) * size)
    units = gate_w.shape[1]
    middle = source_ref[rows, :].astype(jnp.float32) + join_halves(kept_ref, other_ref, work_ref)
    middle_ref[...] = middle
    second = rms_apply(middle, gain_ref[...]).astype(jnp.bfloat16)
    second_ref[...] = second
    gate_pre = product(second, gate_w[...])
    up_pre = product(second, up_w[...])
    bell = jax.nn.sigmoid(gate_pre)
    silu = gate_pre * bell
    hidden = (silu * up_pre).astype(jnp.bfloat16)
    hidden_ref[...] = hidden
    hidden_back = contract(upstream_ref[rows, :], down_w[...], 1, 1, None)
    gate_back = (hidden_back * up_pre * (bell * (1.0 + gate_pre * (1.0 - bell)))).astype(jnp.bfloat16)
    up_back = (hidden_back * silu).astype(jnp.bfloat16)
    back_ref[:, :units] = gate_back
    back_ref[:, units:] = up_back
    terms = contract(gate_back, gate_w[...], 1, 1, None) + contract(up_back, up_w[...], 1, 1, None)
    split_halves(terms, second_sent, second_kept, work_ref)
    split_halves(product(hidden, down_w[...]), output_sent, output_kept, work_ref)


def join_output(*refs):
    out_ref, work_ref = refs[-2:]
    size = out_ref.shape[0] // PARTS
    for part in range(PARTS):
        kept_ref, other_ref, middle_ref = refs[3 * part : 3 * part + 3]
        total = middle_ref[...] + join_halves(kept_ref, other_ref, work_ref)
        out_ref[part * size : (part + 1) * size, :] = total.astype(jnp.bfloat16)


def gate_backward(*refs):
    parts = refs[: 3 * PARTS]
    (
        upstream_ref,
        swiglu_gain_ref,
        weight_ref,
        mixed_ref,
        outgate_ref,
        gain_ref,
        reach_ref,
        middle_round_ref,
        middle_own_ref,
        mixed_back_ref,
        outgate_back_ref,
        group_ref,
        swiglu_ref,
        self_ref,
        work_ref,
        full_ref,
    ) = refs[3 * PARTS :]
    size = work_ref.shape[0]
    swiglu = jnp.zeros_like(swiglu_ref[...])
    for part in range(PARTS):
        kept_ref, other_ref, middle_ref = parts[3 * part : 3 * part + 3]
        rows = slice(part * size, (part + 1) * size)
        second_back = join_halves(kept_ref, other_ref, work_ref)
        middle = middle_ref[...]
        root = lax.rsqrt(jnp.mean(middle * middle, axis=-1, keepdims=True) + EPS)
        unit = middle * root
        swiglu = swiglu + jnp.sum(second_back * unit, axis=0, keepdims=True)
        inner = second_back * swiglu_gain_ref[...]
        back = root * (inner - unit * jnp.mean(inner * unit, axis=-1, keepdims=True))
        back = back + upstream_ref[rows, :].astype(jnp.float32)
        full_ref[rows, :] = back
        middle_round_ref[rows, :] = back.astype(jnp.bfloat16)
    swiglu_ref[...] = swiglu
    width = middle_own_ref.shape[1]
    middle_own_ref[...] = full_ref[:, pl.ds(pl.multiple_of(lax.axis_index("tensor") * width, width), width)]
    heads = mixed_ref.shape[1] // DV
    gated_back = contract(middle_round_ref[...], weight_ref[...], 1, 1, None)
    group = jnp.zeros((1, DV), jnp.float32)
    for head in range(heads):
        narrow = slice(head * DK, (head + 1) * DK)
        wide = slice(head * DV, (head + 1) * DV)
        mixed, gate, back = mixed_ref[:, wide], outgate_ref[:, wide], gated_back[:, wide]
        root = lax.rsqrt(jnp.mean(mixed * mixed, axis=-1, keepdims=True) + EPS)
        bell = jax.nn.sigmoid(gate)
        unit = mixed * root
        outer = back * (gate * bell)
        group = group + jnp.sum(outer * unit, axis=0, keepdims=True)
        outgate_back = back * unit * gain_ref[...] * (bell * (1.0 + gate * (1.0 - bell)))
        outgate_back_ref[:, wide] = outgate_back.astype(jnp.bfloat16)
        inner = outer * gain_ref[...]
        mixed_back = root * (inner - unit * jnp.mean(inner * unit, axis=-1, keepdims=True))
        mixed_back_ref[:, wide] = mixed_back
        self_ref[wide, :] = contract(mixed_back, reach_ref[:, narrow], 0, 0)
    group_ref[...] = group


def input_terms(
    source_ref,
    gain_ref,
    normed_ref,
    query_ref,
    key_ref,
    value_ref,
    outgate_ref,
    lowrank_ref,
    query_w,
    key_w,
    value_w,
    outgate_w,
    down_w,
    group_ref,
    swiglu_ref,
    expand_ref,
    bias_ref,
    shared_ref,
    split_ref,
    own_ref,
    *rest,
):
    steps, full_ref = rest[:-1], rest[-1]
    length, width = source_ref.shape
    terms = contract(query_ref[...], query_w[...], 1, 1, None)
    terms = terms + contract(key_ref[...], key_w[...], 1, 1, None)
    terms = terms + contract(value_ref[...], value_w[...], 1, 1, None)
    terms = terms + contract(outgate_ref[...], outgate_w[...], 1, 1, None)
    terms = terms + contract(lowrank_ref[...], down_w[...], 1, 1, None)
    full_ref[...] = terms
    count = lax.axis_size("tensor")
    place = lax.axis_index("tensor")
    own = width // count

    def block(index):
        return full_ref[:, pl.ds(pl.multiple_of(index * own, own), own)]

    own_ref[...] = block(place)
    for step in range(1, count):
        steps[2 * step - 2][...] = block(jnp.minimum(count - step + place, count - 1))
        steps[2 * step - 1][...] = block(jnp.maximum(place - count + step, 0))
    source = source_ref[...].astype(jnp.float32)
    root = lax.rsqrt(jnp.mean(source * source, axis=-1, keepdims=True) + EPS)
    along = terms * source
    rank = lowrank_ref.shape[1]
    shared_ref[...] = jnp.zeros_like(shared_ref)
    shared_ref[:rank, :] = contract(lowrank_ref[...], normed_ref[...], 0, 0, None)
    shared_ref[rank : rank + 1, :] = jnp.sum(along * root, axis=0, keepdims=True)
    shared_ref[rank + 1 : rank + 2, :DV] = group_ref[...]
    inner = jnp.sum(along * gain_ref[...], axis=-1, keepdims=True)
    shared_ref[rank + 2 : rank + 3, :length] = jnp.broadcast_to(inner, (length, 128)).T[:1]
    split_ref[...] = jnp.zeros_like(split_ref)
    split_ref[:1, :] = swiglu_ref[...]
    keys = bias_ref.shape[1]
    split_ref[1:2, :keys] = bias_ref[...]
    many = width // keys
    for row in range(rank):
        start = row % many * keys
        split_ref[2 + row // many : 3 + row // many, start : start + keys] = expand_ref[row : row + 1, :]


def gradient_blocks(*refs):
    pairs, (sent_ref, kept_ref) = refs[:-2], refs[-2:]
    size = sent_ref.shape[0] // len(ORDER)
    place, own = lax.axis_index("dp"), lax.axis_index("seq")
    for far, out_ref in ((1, sent_ref), (0, kept_ref)):
        for index, step in enumerate(ORDER):
            block = (place ^ step) * 2 + (own ^ far)
            columns = pl.ds(pl.multiple_of(block * size, size), size)
            start = 0
            for left_ref, right_ref in zip(pairs[::2], pairs[1::2]):
                end = start + right_ref.shape[1]
                out_ref[index * size : (index + 1) * size, start:end] = contract(
                    left_ref[:, columns], right_ref[...], 0, 0, None
                )
                start = end


def round_up(count, multiple):
    return -(-count // multiple) * multiple


def gradients(pairs, name):
    columns = sum(right.shape[1] for _, right in pairs)
    width = pairs[0][0].shape[1]
    if direct():
        flat = [array for pair in pairs for array in pair]
        half = shape_of(width // 2, columns)
        flops = 2 * width * columns * pairs[0][0].shape[0]
        sent, kept = call(gradient_blocks, [half, half], flops, name=name)(*flat)
        return jnp.concatenate(scatter_pair(sent, kept), axis=1)
    whole = jnp.concatenate([product(left.T, right) for left, right in pairs], axis=1)
    return lax.psum_scatter(whole, ("dp", "seq"), scatter_dimension=0, tiled=True)


def on_device(
    block_input,
    mixer_gain,
    query_weight,
    key_weight,
    value_weight,
    outgate_weight,
    decay_down,
    decay_up,
    decay_bias,
    group_gain,
    output_weight,
    swiglu_gain,
    gate_weight,
    up_weight,
    down_weight,
    cotangent,
):
    rounded = jnp.bfloat16
    source, upstream = block_input[0], cotangent[0]
    length, width = source.shape
    keys, values, units = query_weight.shape[1], value_weight.shape[1], gate_weight.shape[1]
    heads = keys // DK
    rank = decay_down.shape[1]
    size = length // PARTS
    half = shape_of(size // 2, width)
    work = pltpu.VMEM((size, width), jnp.float32)
    (
        normed,
        query,
        keyrow,
        value,
        outgate,
        lowrank,
        logit,
        cumul,
        reach,
        local,
        local_state,
        decay_total,
    ) = call(
        mix_forward,
        [
            shape_of(length, width, rounded),
            shape_of(length, keys),
            shape_of(length, keys),
            shape_of(length, values),
            shape_of(length, values),
            shape_of(length, rank),
            shape_of(length, keys),
            shape_of(length, keys),
            shape_of(length, keys),
            shape_of(length, values),
            shape_of(values, DK),
            shape_of(heads, DK),
        ],
        2 * length * width * (2 * keys + 2 * values),
        name="mix_forward",
    )(
        source,
        mixer_gain[None],
        query_weight,
        key_weight,
        value_weight,
        outgate_weight,
        decay_down,
        decay_up,
        decay_bias[None],
    )
    decay_rows = jnp.repeat(decay_total, DV, axis=0)
    incoming = relay(local_state, decay_rows, "seq", False)
    mixed, gated, *pieces = call(
        gate_forward,
        [shape_of(length, values), shape_of(length, values, rounded)] + [half] * (2 * PARTS),
        2 * length * width * values,
        scratch=[work],
        name="gate_forward",
    )(local, reach, incoming, outgate, group_gain[None], output_weight)
    parts = []
    for part in range(PARTS):
        kept, other = halves_sum(pieces[2 * part], pieces[2 * part + 1])
        parts.append(
            call(
                functools.partial(feed_forward, part=part),
                [
                    shape_of(size, width),
                    shape_of(size, width, rounded),
                    shape_of(size, units, rounded),
                    shape_of(size, 2 * units, rounded),
                    half,
                    half,
                    half,
                    half,
                ],
                12 * size * width * units,
                scratch=[work],
                name="feed_forward",
            )(kept, other, source, upstream, swiglu_gain[None], gate_weight, up_weight, down_weight)
        )
    second_sums = []
    for part in parts:
        second_sums += [*halves_sum(part[4], part[5]), part[0]]
    second = jnp.concatenate([part[1] for part in parts], axis=0)
    hidden = jnp.concatenate([part[2] for part in parts], axis=0)
    units_back = jnp.concatenate([part[3] for part in parts], axis=0)
    wide_total = gradients([(second, units_back), (upstream, hidden)], "wide_blocks")
    output_sums = []
    for part in parts:
        output_sums += [*halves_sum(part[6], part[7]), part[0]]
    (block_output,) = call(
        join_output, [shape_of(length, width, rounded)], length * width, scratch=[work], name="join_output"
    )(*output_sums)
    count = lax.axis_size("tensor")
    own = width // count
    middle_round, middle_own, mixed_back, outgate_round, group_part, swiglu_part, self_gradient = call(
        gate_backward,
        [
            shape_of(length, width, rounded),
            shape_of(length, own),
            shape_of(length, values),
            shape_of(length, values, rounded),
            shape_of(1, DV),
            shape_of(1, width),
            shape_of(values, DK),
        ],
        2 * length * width * values,
        scratch=[work, pltpu.VMEM((length, width), jnp.float32)],
        name="gate_backward",
    )(*second_sums, upstream, swiglu_gain[None], output_weight, mixed, outgate, group_gain[None], reach)
    outgoing = relay(self_gradient, decay_rows, "seq", True)
    query_round, key_round, value_round, lowrank_round, expand_part, bias_part = call(
        mix_backward,
        [
            shape_of(length, keys, rounded),
            shape_of(length, keys, rounded),
            shape_of(length, values, rounded),
            shape_of(length, rank, rounded),
            shape_of(rank, keys),
            shape_of(1, keys),
        ],
        20 * length * DK * values,
        scratch=[
            pltpu.VMEM((length // SPAN, DV, DK), jnp.float32),
            pltpu.VMEM((length, keys), jnp.float32),
        ],
        name="mix_backward",
    )(query, keyrow, value, cumul, logit, lowrank, mixed_back, incoming, outgoing, decay_up)
    many = width // keys
    split_rows = round_up(2 + round_up(rank, many) // many, 8)
    shared_rows = round_up(rank + 3, 8)
    shared, split, own_terms, *steps = call(
        input_terms,
        [shape_of(shared_rows, width), shape_of(split_rows, width)]
        + [shape_of(length, own)] * (2 * count - 1),
        2 * length * width * (2 * keys + 2 * values),
        scratch=[pltpu.VMEM((length, width), jnp.float32)],
        name="input_terms",
    )(
        source,
        mixer_gain[None],
        normed,
        query_round,
        key_round,
        value_round,
        outgate_round,
        lowrank_round,
        query_weight,
        key_weight,
        value_weight,
        outgate_weight,
        decay_down,
        group_part,
        swiglu_part,
        expand_part,
        bias_part,
    )
    right = left = None
    for step in range(1, count):
        sent = steps[2 * step - 2] if right is None else steps[2 * step - 2] + right
        right = lax.ppermute(sent, "tensor", [(i, i + 1) for i in range(step)])
        sent = steps[2 * step - 1] if left is None else steps[2 * step - 1] + left
        left = lax.ppermute(sent, "tensor", [(count - 1 - i, count - 2 - i) for i in range(step)])
    mixer_total = gradients(
        [
            (normed, query_round),
            (normed, key_round),
            (normed, value_round),
            (normed, outgate_round),
            (middle_round, gated),
        ],
        "mixer_blocks",
    )
    shared = butterfly(shared, "tensor")
    inner = shared[rank + 2, :length][:, None]
    small = jnp.concatenate([shared, split], axis=0)
    small = butterfly(butterfly(small, "seq"), "dp")
    place = lax.axis_index("tensor")
    normed_back = own_terms if right is None else own_terms + right + left
    wide_source = source.astype(jnp.float32)
    root = lax.rsqrt(jnp.mean(wide_source * wide_source, axis=-1, keepdims=True) + EPS)
    source_own = column_block(wide_source, place, own)
    weighted = normed_back * lax.dynamic_slice_in_dim(mixer_gain, place * own, own, 0)
    source_back = root * weighted - source_own * (root * root * root * inner / width)
    mixer_part = lax.dynamic_slice_in_dim(small[rank], place * own, own, 0)
    ends = (keys, 2 * keys, 2 * keys + values, 2 * keys + 2 * values)
    expand_rows = small[shared_rows + 2 : shared_rows + 2 + round_up(rank, many) // many]
    return (
        block_output[None],
        (middle_own + source_back)[None],
        mixer_part,
        mixer_total[:, : ends[0]],
        mixer_total[:, ends[0] : ends[1]],
        mixer_total[:, ends[1] : ends[2]],
        mixer_total[:, ends[2] : ends[3]],
        small[:rank].T,
        expand_rows.reshape(-1, keys)[:rank],
        small[shared_rows + 1, :keys],
        small[rank + 1, :DV],
        mixer_total[:, ends[3] :].T,
        small[shared_rows],
        wide_total[:, :units],
        wide_total[:, units : 2 * units],
        wide_total[:, 2 * units :].T,
    )


def solution(mesh):
    in_specs = (
        P("dp", "seq", None),
        P(),
        P(None, "tensor"),
        P(None, "tensor"),
        P(None, "tensor"),
        P(None, "tensor"),
        P(),
        P(None, "tensor"),
        P("tensor"),
        P(),
        P("tensor", None),
        P(),
        P(None, "tensor"),
        P(None, "tensor"),
        P("tensor", None),
        P("dp", "seq", None),
    )
    out_specs = (
        P("dp", "seq", None),
        P("dp", "seq", "tensor"),
        P("tensor"),
        P(("dp", "seq"), "tensor"),
        P(("dp", "seq"), "tensor"),
        P(("dp", "seq"), "tensor"),
        P(("dp", "seq"), "tensor"),
        P(),
        P(None, "tensor"),
        P("tensor"),
        P(),
        P("tensor", ("dp", "seq")),
        P(),
        P(("dp", "seq"), "tensor"),
        P(("dp", "seq"), "tensor"),
        P("tensor", ("dp", "seq")),
    )
    return jax.shard_map(
        on_device, mesh=mesh, in_specs=in_specs, out_specs=out_specs, check_vma=False
    )
```

```python
import functools

import jax
import jax.numpy as jnp
from jax import lax
from jax.experimental import pallas as pl
from jax.experimental.pallas import tpu as pltpu
from jax.sharding import PartitionSpec as P

DK = 128
DV = 256
SPAN = 64
TILE = 8
PARTS = 2
ORDER = (0, 1, 3, 2)
VMEM_LIMIT = 32 * 2**20


EPS = 1e-06
GATE_NORM = 16.0
highest_precision = lax.Precision.HIGHEST


def flip(values, axis, mask):
    count = lax.axis_size(axis)
    return lax.ppermute(values, axis, [(i, i ^ mask) for i in range(count)])


def butterfly(values, axis, first=1):
    count = lax.axis_size(axis)
    mask = first
    while mask < count:
        values = values + flip(values, axis, mask)
        mask *= 2
    return values


def after(values, *earlier):
    return lax.optimization_barrier((values, *earlier))[0]


def halves_sum(sent, kept, state):
    if lax.axis_size("tensor") == 1:
        return kept, sent
    got = flip(after(sent, *state.get("in", ())), "tensor", 1)
    state["in"] = (got,)
    kept = kept + got
    kept = butterfly(kept, "tensor", 2)
    return kept, flip(kept, "tensor", 1)


def line_gather(own):
    count = lax.axis_size("tensor")
    right = left = own
    blocks = [own]
    for step in range(1, count):
        right = lax.ppermute(right, "tensor", [(i, i + 1) for i in range(step - 1, count - 1)])
        left = lax.ppermute(left, "tensor", [(i + 1, i) for i in range(count - step)])
        blocks += [right, left]
    return blocks


def upper_half():
    return lax.axis_index("tensor") % 2


def column_block(values, block, width):
    return lax.dynamic_slice_in_dim(values, block * width, width, 1)


def direct():
    return lax.axis_size("dp") == 4 and lax.axis_size("seq") == 2


def scatter_start(sent, kept):
    size = kept[0].shape[0] // 4
    one, two = (flip(values, "seq", 1) for values in sent)
    near = slice(size, 3 * size)
    got = flip(kept[0][near] + one[near], "dp", 1)
    near = slice(2 * size, 4 * size)
    far = flip(kept[1][near] + two[near], "dp", 2)
    return kept, (one, two), (got, far)


def scatter_end(kept, sums, moved):
    size = kept[0].shape[0] // 4
    (one, two), (got, far) = sums, moved
    first, last = slice(0, size), slice(3 * size, 4 * size)
    late = flip(kept[0][last] + one[last] + got[size:], "dp", 2)
    done = kept[0][first] + one[first] + got[:size] + late
    near = slice(size, 2 * size)
    late = flip(kept[1][near] + two[near] + far[:size], "dp", 1)
    return done, kept[1][first] + two[first] + far[size:] + late


def product(left, right):
    return jnp.dot(left, right, preferred_element_type=jnp.float32)


def rms_apply(values, gain):
    return values * lax.rsqrt(jnp.mean(values * values, axis=-1, keepdims=True) + EPS) * gain


MIX_PRECISION = lax.Precision.HIGHEST


def contract(left, right, left_dim, right_dim, precision=MIX_PRECISION):
    return lax.dot_general(
        left,
        right,
        (((left_dim,), (right_dim,)), ((), ())),
        precision=precision,
        preferred_element_type=jnp.float32,
    )


def exact(left, right, left_dim, right_dim):
    return contract(left, right, left_dim, right_dim, highest_precision)


def grid_of(shape, dim):
    return lax.broadcasted_iota(jnp.int32, shape, dim)


def level_masks(span):
    row, col = grid_of((span, span), 0), grid_of((span, span), 1)
    masks = []
    half = span // 2
    while half >= TILE:
        masks.append((half, (row // (2 * half) == col // (2 * half)) & (row // half > col // half)))
        half //= 2
    return masks, (row // TILE == col // TILE) & (row >= col), col % TILE


def level_decay(cumul, half):
    rows, width = cumul.shape
    middle = [
        jnp.broadcast_to(cumul[start + half - 1 : start + half], (2 * half, width))
        for start in range(0, rows, 2 * half)
    ]
    return jnp.exp(-jnp.abs(cumul - jnp.concatenate(middle, axis=0)))


def tiles(values):
    return values.reshape(values.shape[0] // TILE, TILE, values.shape[1])


def span_scores(query, keyrow, cumul, masks, near, place):
    span = query.shape[0]
    scores = jnp.zeros((span, span), jnp.float32)
    for half, mask in masks:
        decay = level_decay(cumul, half)
        scores = scores + jnp.where(mask, contract(query * decay, keyrow * decay, 1, 1), 0.0)
    query3, key3, cumul3 = tiles(query), tiles(keyrow), tiles(cumul)
    close = jnp.zeros((span, span), jnp.float32)
    for step in range(TILE):
        decay = jnp.exp(jnp.minimum(cumul3 - cumul3[:, step : step + 1], 0.0))
        terms = (query3 * key3[:, step : step + 1] * decay).reshape(span, -1)
        close = jnp.where(place == step, jnp.sum(terms, axis=-1, keepdims=True), close)
    return scores + jnp.where(near, close, 0.0)


def triangle(span, upper):
    row, col = grid_of((span, span), 0), grid_of((span, span), 1)
    return jnp.where(row <= col if upper else row >= col, 1.0, 0.0).astype(jnp.float32)


def mix_forward(
    source_ref,
    gain_ref,
    query_w,
    key_w,
    value_w,
    outgate_w,
    down_w,
    up_w,
    bias_ref,
    normed_ref,
    query_ref,
    key_ref,
    value_ref,
    outgate_ref,
    lowrank_ref,
    logit_ref,
    cumul_ref,
    reach_ref,
    local_ref,
    state_ref,
    total_ref,
):
    length = source_ref.shape[0]
    heads = query_w.shape[1] // DK
    normed = rms_apply(source_ref[...].astype(jnp.float32), gain_ref[...]).astype(jnp.bfloat16)
    normed_ref[...] = normed
    lowrank = product(normed, down_w[...])
    lowrank_ref[...] = lowrank
    logit = exact(lowrank, up_w[...].astype(jnp.float32), 1, 0) + bias_ref[...]
    logit_ref[...] = logit
    forget = (jnp.minimum(logit, 0.0) - jnp.log1p(jnp.exp(-jnp.abs(logit)))) / GATE_NORM
    query_ref[...] = product(normed, query_w[...])
    key_ref[...] = product(normed, key_w[...])
    value_ref[...] = product(normed, value_w[...])
    outgate_ref[...] = product(normed, outgate_w[...])
    masks, near, place = level_masks(SPAN)
    lower = triangle(SPAN, False)
    scale = DK ** (-0.5)
    for head in range(heads):
        narrow = slice(head * DK, (head + 1) * DK)
        wide = slice(head * DV, (head + 1) * DV)
        state = None
        base = jnp.zeros((1, DK), jnp.float32)
        for start in range(0, length, SPAN):
            rows = slice(start, start + SPAN)
            query, keyrow, value = query_ref[rows, narrow], key_ref[rows, narrow], value_ref[rows, wide]
            cumul = exact(lower, forget[rows, narrow], 1, 0)
            cumul_ref[rows, narrow] = cumul
            last = cumul[SPAN - 1 : SPAN]
            reach_ref[rows, narrow] = query * jnp.exp(cumul + base) * scale
            base = base + last
            scores = span_scores(query, keyrow, cumul, masks, near, place)
            mixed = contract(scores, value, 1, 0)
            if state is not None:
                mixed = mixed + contract(query * jnp.exp(cumul), state, 1, 1)
            local_ref[rows, wide] = mixed * scale
            added = contract(value, keyrow * jnp.exp(last - cumul), 0, 0)
            state = added if state is None else state * jnp.exp(last) + added
        state_ref[wide, :] = state
        total_ref[head : head + 1, :] = jnp.exp(base)


def mix_backward(
    query_ref,
    key_ref,
    value_ref,
    cumul_ref,
    logit_ref,
    lowrank_ref,
    mixed_back_ref,
    state_ref,
    state_back_ref,
    up_w,
    query_back_ref,
    key_back_ref,
    value_back_ref,
    lowrank_back_ref,
    expand_ref,
    bias_ref,
    states_ref,
    logit_back_ref,
):
    length = query_ref.shape[0]
    heads = query_ref.shape[1] // DK
    count = length // SPAN
    masks, near, place = level_masks(SPAN)
    upper = triangle(SPAN, True)
    scale = DK ** (-0.5)
    final = grid_of((SPAN, DK), 0) == SPAN - 1
    lane_row = grid_of((SPAN // TILE, TILE, DK), 1)
    for head in range(heads):
        narrow = slice(head * DK, (head + 1) * DK)
        wide = slice(head * DV, (head + 1) * DV)
        state = state_ref[wide, :]
        for index in range(count):
            rows = slice(index * SPAN, (index + 1) * SPAN)
            states_ref[index] = state
            cumul = cumul_ref[rows, narrow]
            last = cumul[SPAN - 1 : SPAN]
            state = state * jnp.exp(last) + contract(
                value_ref[rows, wide], key_ref[rows, narrow] * jnp.exp(last - cumul), 0, 0
            )
        after = state
        carried = state_back_ref[wide, :]
        for index in reversed(range(count)):
            rows = slice(index * SPAN, (index + 1) * SPAN)
            query, keyrow, value = query_ref[rows, narrow], key_ref[rows, narrow], value_ref[rows, wide]
            cumul = cumul_ref[rows, narrow]
            last = cumul[SPAN - 1 : SPAN]
            back = mixed_back_ref[rows, wide] * scale
            before = states_ref[index]
            grown, rest = jnp.exp(cumul), jnp.exp(last - cumul)
            scores = span_scores(query, keyrow, cumul, masks, near, place)
            value_back = contract(scores, back, 0, 0) + contract(keyrow * rest, carried, 1, 1)
            value_back_ref[rows, wide] = value_back.astype(jnp.bfloat16)
            pairs = contract(back, value, 1, 1)
            query_back = grown * contract(back, before, 1, 0)
            key_back = rest * contract(value, carried, 1, 0)
            for half, mask in masks:
                decay = level_decay(cumul, half)
                chosen = jnp.where(mask, pairs, 0.0)
                query_back = query_back + decay * contract(chosen, keyrow * decay, 1, 0)
                key_back = key_back + decay * contract(chosen, query * decay, 0, 0)
            close = jnp.where(near, pairs, 0.0)
            query3, key3, cumul3 = tiles(query), tiles(keyrow), tiles(cumul)
            query_near = jnp.zeros_like(query3)
            key_near = jnp.zeros_like(key3)
            for step in range(TILE):
                column = jnp.sum(jnp.where(place == step, close, 0.0), axis=-1, keepdims=True)
                decay = jnp.exp(jnp.minimum(cumul3 - cumul3[:, step : step + 1], 0.0))
                weight = tiles(jnp.broadcast_to(column, (SPAN, DK))) * decay
                query_near = query_near + weight * key3[:, step : step + 1]
                total = jnp.sum(weight * query3, axis=1, keepdims=True)
                key_near = jnp.where(lane_row == step, total, key_near)
            query_back = query_back + query_near.reshape(SPAN, DK)
            key_back = key_back + key_near.reshape(SPAN, DK)
            query_back_ref[rows, narrow] = query_back.astype(jnp.bfloat16)
            key_back_ref[rows, narrow] = key_back.astype(jnp.bfloat16)
            cumul_back = query * query_back - keyrow * key_back
            ending = jnp.sum(after * carried, axis=0, keepdims=True)
            cumul_back = cumul_back + jnp.where(final, ending, 0.0)
            forget_back = exact(upper, cumul_back, 1, 0)
            logit_back_ref[rows, narrow] = forget_back * jax.nn.sigmoid(-logit_ref[rows, narrow]) / GATE_NORM
            carried = carried * jnp.exp(last) + contract(back, query * grown, 0, 0)
            after = before
    logit_back = logit_back_ref[...]
    lowrank_back_ref[...] = exact(logit_back, up_w[...].astype(jnp.float32), 1, 1).astype(jnp.bfloat16)
    expand_ref[...] = exact(lowrank_ref[...], logit_back, 0, 0)
    bias_ref[...] = jnp.sum(logit_back, axis=0, keepdims=True)


def call(kernel, outs, flops, scratch=()):
    whole = pl.BlockSpec(memory_space=pltpu.VMEM)

    def run(*args):
        moved = sum(a.size * a.dtype.itemsize for a in args)
        moved += sum(o.size * o.dtype.itemsize for o in outs)
        return pl.pallas_call(
            kernel,
            out_shape=tuple(outs),
            in_specs=[whole] * len(args),
            out_specs=tuple([whole] * len(outs)),
            scratch_shapes=list(scratch),
            compiler_params=pltpu.CompilerParams(vmem_limit_bytes=VMEM_LIMIT),
            cost_estimate=pl.CostEstimate(flops=flops, bytes_accessed=moved, transcendentals=0),
        )(*args)

    return run


def shape_of(rows, cols, kind=jnp.float32):
    return jax.ShapeDtypeStruct((rows, cols), kind)


def relay(own, total, axis, reverse):
    count = lax.axis_size(axis)
    pairs = [(i + 1, i) if reverse else (i, i + 1) for i in range(count - 1)]
    entering = None
    for _ in range(count - 1):
        sent = own if entering is None else own + total * entering
        entering = lax.ppermute(sent, axis, pairs)
    return jnp.zeros_like(own) if entering is None else entering


def split_halves(value, sent_ref, kept_ref, work_ref):
    half = value.shape[0] // 2
    work_ref[...] = value
    upper = upper_half()
    kept_ref[...] = work_ref[pl.ds(pl.multiple_of(upper * half, half), half), :]
    sent_ref[...] = work_ref[pl.ds(pl.multiple_of((1 - upper) * half, half), half), :]


def join_halves(kept_ref, other_ref, work_ref):
    half = kept_ref.shape[0]
    upper = upper_half()
    work_ref[pl.ds(pl.multiple_of(upper * half, half), half), :] = kept_ref[...]
    work_ref[pl.ds(pl.multiple_of((1 - upper) * half, half), half), :] = other_ref[...]
    return work_ref[...]


def gate_forward(local_ref, reach_ref, state_ref, outgate_ref, gain_ref, mixed_ref, gated_ref, sent_ref):
    heads = local_ref.shape[1] // DV
    for head in range(heads):
        narrow = slice(head * DK, (head + 1) * DK)
        wide = slice(head * DV, (head + 1) * DV)
        mixed = local_ref[:, wide] + contract(reach_ref[:, narrow], state_ref[wide, :], 1, 1)
        mixed_ref[:, wide] = mixed
        gate = outgate_ref[:, wide]
        gated = rms_apply(mixed, gain_ref[...]) * (gate * jax.nn.sigmoid(gate))
        gated_ref[:, wide] = gated.astype(jnp.bfloat16)
    sent_ref[...] = gated_ref[...].astype(jnp.float32)


def feed_forward(
    *refs,
    part,
):
    count = lax.axis_size("tensor")
    place = lax.axis_index("tensor")
    heads, output_w = refs[: 2 * count - 1], refs[2 * count - 1]
    size = heads[0].shape[0] // PARTS
    rows = slice(part * size, (part + 1) * size)
    span = heads[0].shape[1]
    attended = jnp.zeros((size, output_w.shape[1]), jnp.float32)
    for index, head_ref in enumerate(heads):
        step = (index + 1) // 2
        block = jnp.maximum(place - step, 0) if index % 2 else jnp.minimum(place + step, count - 1)
        weight = output_w[pl.ds(pl.multiple_of(block * span, span), span), :].astype(jnp.bfloat16)
        attended = attended + product(head_ref[rows, :].astype(jnp.bfloat16), weight)
    feed_forward_part(attended, rows, *refs[2 * count :])


def feed_forward_part(
    attended,
    rows,
    source_ref,
    upstream_ref,
    gain_ref,
    gate_w,
    up_w,
    down_w,
    middle_ref,
    second_ref,
    hidden_ref,
    back_ref,
    second_sent,
    second_kept,
    output_sent,
    output_kept,
    work_ref,
):
    units = gate_w.shape[1]
    middle = source_ref[rows, :].astype(jnp.float32) + attended
    middle_ref[...] = middle
    second = rms_apply(middle, gain_ref[...]).astype(jnp.bfloat16)
    second_ref[...] = second
    gate_pre = product(second, gate_w[...])
    up_pre = product(second, up_w[...])
    bell = jax.nn.sigmoid(gate_pre)
    silu = gate_pre * bell
    hidden = (silu * up_pre).astype(jnp.bfloat16)
    hidden_ref[...] = hidden
    hidden_back = contract(upstream_ref[rows, :], down_w[...], 1, 1, None)
    gate_back = (hidden_back * up_pre * (bell * (1.0 + gate_pre * (1.0 - bell)))).astype(jnp.bfloat16)
    up_back = (hidden_back * silu).astype(jnp.bfloat16)
    back_ref[:, :units] = gate_back
    back_ref[:, units:] = up_back
    terms = contract(gate_back, gate_w[...], 1, 1, None) + contract(up_back, up_w[...], 1, 1, None)
    split_halves(terms, second_sent, second_kept, work_ref)
    split_halves(product(hidden, down_w[...]), output_sent, output_kept, work_ref)


def join_output(*refs):
    out_ref, work_ref = refs[-2:]
    size = out_ref.shape[0] // PARTS
    for part in range(PARTS):
        kept_ref, other_ref, middle_ref = refs[3 * part : 3 * part + 3]
        total = middle_ref[...] + join_halves(kept_ref, other_ref, work_ref)
        out_ref[part * size : (part + 1) * size, :] = total.astype(jnp.bfloat16)


def gate_backward(*refs):
    parts = refs[: 3 * PARTS]
    (
        upstream_ref,
        swiglu_gain_ref,
        weight_ref,
        mixed_ref,
        outgate_ref,
        gain_ref,
        reach_ref,
        middle_round_ref,
        middle_own_ref,
        mixed_back_ref,
        outgate_back_ref,
        group_ref,
        swiglu_ref,
        self_ref,
        work_ref,
        full_ref,
    ) = refs[3 * PARTS :]
    size = work_ref.shape[0]
    swiglu = jnp.zeros_like(swiglu_ref[...])
    for part in range(PARTS):
        kept_ref, other_ref, middle_ref = parts[3 * part : 3 * part + 3]
        rows = slice(part * size, (part + 1) * size)
        second_back = join_halves(kept_ref, other_ref, work_ref)
        middle = middle_ref[...]
        root = lax.rsqrt(jnp.mean(middle * middle, axis=-1, keepdims=True) + EPS)
        unit = middle * root
        swiglu = swiglu + jnp.sum(second_back * unit, axis=0, keepdims=True)
        inner = second_back * swiglu_gain_ref[...]
        back = root * (inner - unit * jnp.mean(inner * unit, axis=-1, keepdims=True))
        back = back + upstream_ref[rows, :].astype(jnp.float32)
        full_ref[rows, :] = back
        middle_round_ref[rows, :] = back.astype(jnp.bfloat16)
    swiglu_ref[...] = swiglu
    width = middle_own_ref.shape[1]
    middle_own_ref[...] = full_ref[:, pl.ds(pl.multiple_of(lax.axis_index("tensor") * width, width), width)]
    heads = mixed_ref.shape[1] // DV
    gated_back = contract(middle_round_ref[...], weight_ref[...], 1, 1, None)
    group = jnp.zeros((1, DV), jnp.float32)
    for head in range(heads):
        narrow = slice(head * DK, (head + 1) * DK)
        wide = slice(head * DV, (head + 1) * DV)
        mixed, gate, back = mixed_ref[:, wide], outgate_ref[:, wide], gated_back[:, wide]
        root = lax.rsqrt(jnp.mean(mixed * mixed, axis=-1, keepdims=True) + EPS)
        bell = jax.nn.sigmoid(gate)
        unit = mixed * root
        outer = back * (gate * bell)
        group = group + jnp.sum(outer * unit, axis=0, keepdims=True)
        outgate_back = back * unit * gain_ref[...] * (bell * (1.0 + gate * (1.0 - bell)))
        outgate_back_ref[:, wide] = outgate_back.astype(jnp.bfloat16)
        inner = outer * gain_ref[...]
        mixed_back = root * (inner - unit * jnp.mean(inner * unit, axis=-1, keepdims=True))
        mixed_back_ref[:, wide] = mixed_back
        self_ref[wide, :] = contract(mixed_back, reach_ref[:, narrow], 0, 0)
    group_ref[...] = group


def input_terms(
    source_ref,
    gain_ref,
    normed_ref,
    query_ref,
    key_ref,
    value_ref,
    outgate_ref,
    lowrank_ref,
    query_w,
    key_w,
    value_w,
    outgate_w,
    down_w,
    group_ref,
    swiglu_ref,
    expand_ref,
    bias_ref,
    small_ref,
    inner_ref,
    own_ref,
    *rest,
):
    steps, full_ref = rest[:-1], rest[-1]
    length, width = source_ref.shape
    terms = contract(query_ref[...], query_w[...], 1, 1, None)
    terms = terms + contract(key_ref[...], key_w[...], 1, 1, None)
    terms = terms + contract(value_ref[...], value_w[...], 1, 1, None)
    terms = terms + contract(outgate_ref[...], outgate_w[...], 1, 1, None)
    terms = terms + contract(lowrank_ref[...], down_w[...], 1, 1, None)
    full_ref[...] = terms
    count = lax.axis_size("tensor")
    place = lax.axis_index("tensor")
    own = width // count

    def block(index):
        return full_ref[:, pl.ds(pl.multiple_of(index * own, own), own)]

    own_ref[...] = block(place)
    for step in range(1, count):
        steps[2 * step - 2][...] = block(jnp.minimum(count - step + place, count - 1))
        steps[2 * step - 1][...] = block(jnp.maximum(place - count + step, 0))
    source = source_ref[...].astype(jnp.float32)
    root = lax.rsqrt(jnp.mean(source * source, axis=-1, keepdims=True) + EPS)
    along = terms * source
    rank = lowrank_ref.shape[1]
    small_ref[...] = jnp.zeros_like(small_ref)
    small_ref[:rank, :] = contract(lowrank_ref[...], normed_ref[...], 0, 0, None)
    small_ref[rank : rank + 1, :] = jnp.sum(along * root, axis=0, keepdims=True)
    small_ref[rank + 1 : rank + 2, :DV] = group_ref[...]
    inner = jnp.sum(along * gain_ref[...], axis=-1, keepdims=True)
    inner_ref[...] = jnp.broadcast_to(inner, (length, 128)).T[: inner_ref.shape[0]]
    base = round_up(rank + 2, 8)
    small_ref[base : base + 1, :] = swiglu_ref[...]
    keys = bias_ref.shape[1]
    small_ref[base + 1 : base + 2, :keys] = bias_ref[...]
    many = width // keys
    for row in range(rank):
        start = row % many * keys
        line = base + 2 + row // many
        small_ref[line : line + 1, start : start + keys] = expand_ref[row : row + 1, :]


def gradient_terms(*refs):
    pairs, out_ref = refs[:-1], refs[-1]
    start = 0
    for left_ref, right_ref in zip(pairs[::2], pairs[1::2]):
        end = start + right_ref.shape[1]
        out_ref[:, start:end] = contract(left_ref[...], right_ref[...], 0, 0, None)
        start = end
    if start < out_ref.shape[1]:
        out_ref[:, start:] = jnp.zeros((out_ref.shape[0], out_ref.shape[1] - start), jnp.float32)


def round_up(count, multiple):
    return -(-count // multiple) * multiple


def gradients(pairs):
    columns = sum(right.shape[1] for _, right in pairs)
    width = pairs[0][0].shape[1]
    flat = [array for pair in pairs for array in pair]
    flops = 2 * width * columns * pairs[0][0].shape[0]
    (terms,) = call(gradient_terms, [shape_of(width, round_up(columns, 128))], flops)(*flat)
    return lax.psum_scatter(terms, ("dp", "seq"), scatter_dimension=0, tiled=True)


def gradient_blocks(*refs):
    pairs, outs = refs[:-4], refs[-4:]
    size = outs[0].shape[0] // len(ORDER)
    cut = outs[0].shape[1]
    place, own = lax.axis_index("dp"), lax.axis_index("seq")
    for far, (one_ref, two_ref) in ((1, outs[:2]), (0, outs[2:])):
        for index, step in enumerate(ORDER):
            block = (place ^ step) * 2 + (own ^ far)
            columns = pl.ds(pl.multiple_of(block * size, size), size)
            rows = slice(index * size, (index + 1) * size)
            start = 0
            for left_ref, right_ref in zip(pairs[::2], pairs[1::2]):
                count = right_ref.shape[1]
                block_sum = contract(left_ref[:, columns], right_ref[...], 0, 0, None)
                here = min(max(cut - start, 0), count)
                if here > 0:
                    one_ref[rows, start : start + here] = block_sum[:, :here]
                if here < count:
                    two_ref[rows, start + here - cut : start + count - cut] = block_sum[:, here:]
                start += count
            if start < cut + two_ref.shape[1]:
                two_ref[rows, start - cut :] = jnp.zeros((size, cut + two_ref.shape[1] - start), jnp.float32)


def gradient_start(pairs):
    columns = sum(right.shape[1] for _, right in pairs)
    width = pairs[0][0].shape[1]
    if direct():
        flat = [array for pair in pairs for array in pair]
        columns = round_up(columns, 128)
        cut = columns // 256 * 128
        halves = [shape_of(width // 2, cut), shape_of(width // 2, columns - cut)]
        flops = 2 * width * columns * pairs[0][0].shape[0]
        outs = call(gradient_blocks, halves * 2, flops)(*flat)
        return scatter_start(outs[:2], outs[2:])
    whole = jnp.concatenate([product(left.T, right) for left, right in pairs], axis=1)
    return lax.psum_scatter(whole, ("dp", "seq"), scatter_dimension=0, tiled=True)


def gradient_end(begun):
    return jnp.concatenate(scatter_end(*begun), axis=1) if direct() else begun


def on_device(
    block_input,
    mixer_gain,
    query_weight,
    key_weight,
    value_weight,
    outgate_weight,
    decay_down,
    decay_up,
    decay_bias,
    group_gain,
    output_weight,
    swiglu_gain,
    gate_weight,
    up_weight,
    down_weight,
    cotangent,
):
    rounded = jnp.bfloat16
    source, upstream = block_input[0], cotangent[0]
    length, width = source.shape
    keys, values, units = query_weight.shape[1], value_weight.shape[1], gate_weight.shape[1]
    heads = keys // DK
    rank = decay_down.shape[1]
    size = length // PARTS
    half = shape_of(size // 2, width)
    work = pltpu.VMEM((size, width), jnp.float32)
    state = {}
    share = values // (lax.axis_size("dp") * lax.axis_size("seq"))
    place = lax.axis_index("dp") * lax.axis_size("seq") + lax.axis_index("seq")
    share_rows = lax.dynamic_slice_in_dim(output_weight, place * share, share, 0).astype(jnp.float32)
    full_output_weight = lax.all_gather(share_rows, ("tensor", "dp", "seq"), axis=0, tiled=True)
    (
        normed,
        query,
        keyrow,
        value,
        outgate,
        lowrank,
        logit,
        cumul,
        reach,
        local,
        local_state,
        decay_total,
    ) = call(
        mix_forward,
        [
            shape_of(length, width, rounded),
            shape_of(length, keys),
            shape_of(length, keys),
            shape_of(length, values),
            shape_of(length, values),
            shape_of(length, rank),
            shape_of(length, keys),
            shape_of(length, keys),
            shape_of(length, keys),
            shape_of(length, values),
            shape_of(values, DK),
            shape_of(heads, DK),
        ],
        2 * length * width * (2 * keys + 2 * values),
    )(
        source,
        mixer_gain[None],
        query_weight,
        key_weight,
        value_weight,
        outgate_weight,
        decay_down,
        decay_up,
        decay_bias[None],
    )
    decay_rows = jnp.repeat(decay_total, DV, axis=0)
    incoming = relay(local_state, decay_rows, "seq", False)
    mixed, gated, sent = call(
        gate_forward,
        [shape_of(length, values), shape_of(length, values, rounded), shape_of(length, values)],
        20 * length * values,
    )(local, reach, incoming, outgate, group_gain[None])
    heads_out = line_gather(sent)
    parts = []
    for part in range(PARTS):
        parts.append(
            call(
                functools.partial(feed_forward, part=part),
                [
                    shape_of(size, width),
                    shape_of(size, width, rounded),
                    shape_of(size, units, rounded),
                    shape_of(size, 2 * units, rounded),
                    half,
                    half,
                    half,
                    half,
                ],
                12 * size * width * units,
                scratch=[work],
            )(*heads_out, full_output_weight, source, upstream, swiglu_gain[None], gate_weight, up_weight, down_weight)
        )
    second_sums = []
    for part in parts:
        second_sums += [*halves_sum(part[4], part[5], state), part[0]]
    second = jnp.concatenate([part[1] for part in parts], axis=0)
    hidden = jnp.concatenate([part[2] for part in parts], axis=0)
    units_back = jnp.concatenate([part[3] for part in parts], axis=0)
    wide_total = gradients([(second, units_back), (upstream, hidden)])
    output_sums = []
    for part in parts:
        output_sums += [*halves_sum(part[6], part[7], state), part[0]]
    (block_output,) = call(
        join_output, [shape_of(length, width, rounded)], length * width, scratch=[work]
    )(*output_sums)
    count = lax.axis_size("tensor")
    own = width // count
    middle_round, middle_own, mixed_back, outgate_round, group_part, swiglu_part, self_gradient = call(
        gate_backward,
        [
            shape_of(length, width, rounded),
            shape_of(length, own),
            shape_of(length, values),
            shape_of(length, values, rounded),
            shape_of(1, DV),
            shape_of(1, width),
            shape_of(values, DK),
        ],
        2 * length * width * values,
        scratch=[work, pltpu.VMEM((length, width), jnp.float32)],
    )(*second_sums, upstream, swiglu_gain[None], output_weight, mixed, outgate, group_gain[None], reach)
    outgoing = relay(self_gradient, decay_rows, "seq", True)
    query_round, key_round, value_round, lowrank_round, expand_part, bias_part = call(
        mix_backward,
        [
            shape_of(length, keys, rounded),
            shape_of(length, keys, rounded),
            shape_of(length, values, rounded),
            shape_of(length, rank, rounded),
            shape_of(rank, keys),
            shape_of(1, keys),
        ],
        20 * length * DK * values,
        scratch=[
            pltpu.VMEM((length // SPAN, DV, DK), jnp.float32),
            pltpu.VMEM((length, keys), jnp.float32),
        ],
    )(query, keyrow, value, cumul, logit, lowrank, mixed_back, incoming, outgoing, decay_up)
    many = width // keys
    split_rows = round_up(2 + round_up(rank, many) // many, 8)
    shared_rows = round_up(rank + 2, 8)
    small, inner, own_terms, *steps = call(
        input_terms,
        [shape_of(shared_rows + split_rows, width), shape_of(8, length)]
        + [shape_of(length, own)] * (2 * count - 1),
        2 * length * width * (2 * keys + 2 * values),
        scratch=[pltpu.VMEM((length, width), jnp.float32)],
    )(
        source,
        mixer_gain[None],
        normed,
        query_round,
        key_round,
        value_round,
        outgate_round,
        lowrank_round,
        query_weight,
        key_weight,
        value_weight,
        outgate_weight,
        decay_down,
        group_part,
        swiglu_part,
        expand_part,
        bias_part,
    )
    right = left = None
    for step in range(1, count):
        sent = steps[2 * step - 2] if right is None else steps[2 * step - 2] + right
        right = lax.ppermute(sent, "tensor", [(i, i + 1) for i in range(step)])
        sent = steps[2 * step - 1] if left is None else steps[2 * step - 1] + left
        left = lax.ppermute(sent, "tensor", [(count - 1 - i, count - 2 - i) for i in range(step)])
    mixer_begun = gradient_start(
        [
            (normed, query_round),
            (normed, key_round),
            (normed, value_round),
            (normed, outgate_round),
            (middle_round, gated),
        ],
    )
    mixer_total = gradient_end(mixer_begun)
    inner = butterfly(inner, "tensor")[0][:, None]
    small = butterfly(small, "seq")
    small = butterfly(small, "dp")
    shared = butterfly(small[:shared_rows], "tensor")
    place = lax.axis_index("tensor")
    normed_back = own_terms if right is None else own_terms + right + left
    wide_source = source.astype(jnp.float32)
    root = lax.rsqrt(jnp.mean(wide_source * wide_source, axis=-1, keepdims=True) + EPS)
    source_own = column_block(wide_source, place, own)
    weighted = normed_back * lax.dynamic_slice_in_dim(mixer_gain, place * own, own, 0)
    source_back = root * weighted - source_own * (root * root * root * inner / width)
    mixer_part = lax.dynamic_slice_in_dim(shared[rank], place * own, own, 0)
    ends = (keys, 2 * keys, 2 * keys + values, 2 * keys + 2 * values)
    expand_rows = small[shared_rows + 2 : shared_rows + 2 + round_up(rank, many) // many]
    return (
        block_output[None],
        (middle_own + source_back)[None],
        mixer_part,
        mixer_total[:, : ends[0]],
        mixer_total[:, ends[0] : ends[1]],
        mixer_total[:, ends[1] : ends[2]],
        mixer_total[:, ends[2] : ends[3]],
        shared[:rank].T,
        expand_rows.reshape(-1, keys)[:rank],
        small[shared_rows + 1, :keys],
        shared[rank + 1, :DV],
        mixer_total[:, ends[3] :].T,
        small[shared_rows],
        wide_total[:, :units],
        wide_total[:, units : 2 * units],
        wide_total[:, 2 * units : 3 * units].T,
    )


def solution(mesh):
    in_specs = (
        P("dp", "seq", None),
        P(),
        P(None, "tensor"),
        P(None, "tensor"),
        P(None, "tensor"),
        P(None, "tensor"),
        P(),
        P(None, "tensor"),
        P("tensor"),
        P(),
        P("tensor", None),
        P(),
        P(None, "tensor"),
        P(None, "tensor"),
        P("tensor", None),
        P("dp", "seq", None),
    )
    out_specs = (
        P("dp", "seq", None),
        P("dp", "seq", "tensor"),
        P("tensor"),
        P(("dp", "seq"), "tensor"),
        P(("dp", "seq"), "tensor"),
        P(("dp", "seq"), "tensor"),
        P(("dp", "seq"), "tensor"),
        P(),
        P(None, "tensor"),
        P("tensor"),
        P(),
        P("tensor", ("dp", "seq")),
        P(),
        P(("dp", "seq"), "tensor"),
        P(("dp", "seq"), "tensor"),
        P("tensor", ("dp", "seq")),
    )
    return jax.shard_map(on_device, mesh=mesh, in_specs=in_specs, out_specs=out_specs, check_vma=False)
```

```python
import functools

import jax
import jax.numpy as jnp
from jax import lax
from jax.experimental import pallas as pl
from jax.experimental.pallas import tpu as pltpu
from jax.sharding import PartitionSpec as P

DK = 128
DV = 256
SPAN = 64
TILE = 8
PARTS = 2
ORDER = (0, 1, 3, 2)
VMEM_LIMIT = 32 * 2**20


EPS = 1e-06
GATE_NORM = 16.0
highest_precision = lax.Precision.HIGHEST


def flip(values, axis, mask):
    count = lax.axis_size(axis)
    return lax.ppermute(values, axis, [(i, i ^ mask) for i in range(count)])


def butterfly(values, axis, first=1):
    count = lax.axis_size(axis)
    mask = first
    while mask < count:
        values = values + flip(values, axis, mask)
        mask *= 2
    return values


def after(values, *earlier):
    return lax.optimization_barrier((values, *earlier))[0]


def halves_sum(sent, kept, state):
    if lax.axis_size("tensor") == 1:
        return kept, sent
    got = flip(after(sent, *state.get("in", ())), "tensor", 1)
    state["in"] = (got,)
    kept = kept + got
    kept = butterfly(kept, "tensor", 2)
    return kept, flip(kept, "tensor", 1)


def line_gather(own):
    count = lax.axis_size("tensor")
    right = left = own
    blocks = [own]
    for step in range(1, count):
        right = lax.ppermute(right, "tensor", [(i, i + 1) for i in range(step - 1, count - 1)])
        left = lax.ppermute(left, "tensor", [(i + 1, i) for i in range(count - step)])
        blocks += [right, left]
    return blocks


def upper_half():
    return lax.axis_index("tensor") % 2


def column_block(values, block, width):
    return lax.dynamic_slice_in_dim(values, block * width, width, 1)


def direct():
    return lax.axis_size("dp") == 4 and lax.axis_size("seq") == 2


def scatter_start(sent, kept):
    size = kept[0].shape[0] // 4
    one, two = (flip(values, "seq", 1) for values in sent)
    near = slice(size, 3 * size)
    got = flip(kept[0][near] + one[near], "dp", 1)
    near = slice(2 * size, 4 * size)
    far = flip(kept[1][near] + two[near], "dp", 2)
    return kept, (one, two), (got, far)


def scatter_end(kept, sums, moved):
    size = kept[0].shape[0] // 4
    (one, two), (got, far) = sums, moved
    first, last = slice(0, size), slice(3 * size, 4 * size)
    late = flip(kept[0][last] + one[last] + got[size:], "dp", 2)
    done = kept[0][first] + one[first] + got[:size] + late
    near = slice(size, 2 * size)
    late = flip(kept[1][near] + two[near] + far[:size], "dp", 1)
    return done, kept[1][first] + two[first] + far[size:] + late


def product(left, right):
    return jnp.dot(left, right, preferred_element_type=jnp.float32)


def rms_apply(values, gain):
    return values * lax.rsqrt(jnp.mean(values * values, axis=-1, keepdims=True) + EPS) * gain


MIX_PRECISION = lax.Precision.HIGHEST


def contract(left, right, left_dim, right_dim, precision=MIX_PRECISION):
    return lax.dot_general(
        left,
        right,
        (((left_dim,), (right_dim,)), ((), ())),
        precision=precision,
        preferred_element_type=jnp.float32,
    )


def exact(left, right, left_dim, right_dim):
    return contract(left, right, left_dim, right_dim, highest_precision)


def grid_of(shape, dim):
    return lax.broadcasted_iota(jnp.int32, shape, dim)


def level_masks(span):
    row, col = grid_of((span, span), 0), grid_of((span, span), 1)
    masks = []
    half = span // 2
    while half >= TILE:
        masks.append((half, (row // (2 * half) == col // (2 * half)) & (row // half > col // half)))
        half //= 2
    return masks, (row // TILE == col // TILE) & (row >= col), col % TILE


def level_decay(cumul, half):
    rows, width = cumul.shape
    middle = [
        jnp.broadcast_to(cumul[start + half - 1 : start + half], (2 * half, width))
        for start in range(0, rows, 2 * half)
    ]
    return jnp.exp(-jnp.abs(cumul - jnp.concatenate(middle, axis=0)))


def tiles(values):
    return values.reshape(values.shape[0] // TILE, TILE, values.shape[1])


def span_scores(query, keyrow, cumul, masks, near, place):
    span = query.shape[0]
    scores = jnp.zeros((span, span), jnp.float32)
    for half, mask in masks:
        decay = level_decay(cumul, half)
        scores = scores + jnp.where(mask, contract(query * decay, keyrow * decay, 1, 1), 0.0)
    query3, key3, cumul3 = tiles(query), tiles(keyrow), tiles(cumul)
    close = jnp.zeros((span, span), jnp.float32)
    for step in range(TILE):
        decay = jnp.exp(jnp.minimum(cumul3 - cumul3[:, step : step + 1], 0.0))
        terms = (query3 * key3[:, step : step + 1] * decay).reshape(span, -1)
        close = jnp.where(place == step, jnp.sum(terms, axis=-1, keepdims=True), close)
    return scores + jnp.where(near, close, 0.0)


def triangle(span, upper):
    row, col = grid_of((span, span), 0), grid_of((span, span), 1)
    return jnp.where(row <= col if upper else row >= col, 1.0, 0.0).astype(jnp.float32)


def mix_forward(
    source_ref,
    gain_ref,
    query_w,
    key_w,
    value_w,
    outgate_w,
    down_w,
    up_w,
    bias_ref,
    normed_ref,
    query_ref,
    key_ref,
    value_ref,
    outgate_ref,
    lowrank_ref,
    logit_ref,
    cumul_ref,
    reach_ref,
    local_ref,
    state_ref,
    total_ref,
):
    length = source_ref.shape[0]
    heads = query_w.shape[1] // DK
    normed = rms_apply(source_ref[...].astype(jnp.float32), gain_ref[...]).astype(jnp.bfloat16)
    normed_ref[...] = normed
    lowrank = contract(normed, down_w[...], 1, 1, None)
    lowrank_ref[...] = lowrank
    logit = exact(lowrank, up_w[...].astype(jnp.float32), 1, 0) + bias_ref[...]
    logit_ref[...] = logit
    forget = (jnp.minimum(logit, 0.0) - jnp.log1p(jnp.exp(-jnp.abs(logit)))) / GATE_NORM
    query_ref[...] = product(normed, query_w[...])
    key_ref[...] = product(normed, key_w[...])
    value_ref[...] = product(normed, value_w[...])
    outgate_ref[...] = product(normed, outgate_w[...])
    masks, near, place = level_masks(SPAN)
    lower = triangle(SPAN, False)
    scale = DK ** (-0.5)
    for head in range(heads):
        narrow = slice(head * DK, (head + 1) * DK)
        wide = slice(head * DV, (head + 1) * DV)
        state = None
        base = jnp.zeros((1, DK), jnp.float32)
        for start in range(0, length, SPAN):
            rows = slice(start, start + SPAN)
            query, keyrow, value = query_ref[rows, narrow], key_ref[rows, narrow], value_ref[rows, wide]
            cumul = exact(lower, forget[rows, narrow], 1, 0)
            cumul_ref[rows, narrow] = cumul
            last = cumul[SPAN - 1 : SPAN]
            reach_ref[rows, narrow] = query * jnp.exp(cumul + base) * scale
            base = base + last
            scores = span_scores(query, keyrow, cumul, masks, near, place)
            mixed = contract(scores, value, 1, 0)
            if state is not None:
                mixed = mixed + contract(query * jnp.exp(cumul), state, 1, 1)
            local_ref[rows, wide] = mixed * scale
            added = contract(value, keyrow * jnp.exp(last - cumul), 0, 0)
            state = added if state is None else state * jnp.exp(last) + added
        state_ref[wide, :] = state
        total_ref[head : head + 1, :] = jnp.exp(base)


def mix_backward(
    query_ref,
    key_ref,
    value_ref,
    cumul_ref,
    logit_ref,
    lowrank_ref,
    mixed_back_ref,
    state_ref,
    state_back_ref,
    up_w,
    query_back_ref,
    key_back_ref,
    value_back_ref,
    lowrank_back_ref,
    expand_ref,
    bias_ref,
    states_ref,
    logit_back_ref,
):
    length = query_ref.shape[0]
    heads = query_ref.shape[1] // DK
    count = length // SPAN
    masks, near, place = level_masks(SPAN)
    upper = triangle(SPAN, True)
    scale = DK ** (-0.5)
    final = grid_of((SPAN, DK), 0) == SPAN - 1
    lane_row = grid_of((SPAN // TILE, TILE, DK), 1)
    for head in range(heads):
        narrow = slice(head * DK, (head + 1) * DK)
        wide = slice(head * DV, (head + 1) * DV)
        state = state_ref[wide, :]
        for index in range(count):
            rows = slice(index * SPAN, (index + 1) * SPAN)
            states_ref[index] = state
            cumul = cumul_ref[rows, narrow]
            last = cumul[SPAN - 1 : SPAN]
            state = state * jnp.exp(last) + contract(
                value_ref[rows, wide], key_ref[rows, narrow] * jnp.exp(last - cumul), 0, 0
            )
        after = state
        carried = state_back_ref[wide, :]
        for index in reversed(range(count)):
            rows = slice(index * SPAN, (index + 1) * SPAN)
            query, keyrow, value = query_ref[rows, narrow], key_ref[rows, narrow], value_ref[rows, wide]
            cumul = cumul_ref[rows, narrow]
            last = cumul[SPAN - 1 : SPAN]
            back = mixed_back_ref[rows, wide] * scale
            before = states_ref[index]
            grown, rest = jnp.exp(cumul), jnp.exp(last - cumul)
            scores = span_scores(query, keyrow, cumul, masks, near, place)
            value_back = contract(scores, back, 0, 0) + contract(keyrow * rest, carried, 1, 1)
            value_back_ref[rows, wide] = value_back.astype(jnp.bfloat16)
            pairs = contract(back, value, 1, 1)
            query_back = grown * contract(back, before, 1, 0)
            key_back = rest * contract(value, carried, 1, 0)
            for half, mask in masks:
                decay = level_decay(cumul, half)
                chosen = jnp.where(mask, pairs, 0.0)
                query_back = query_back + decay * contract(chosen, keyrow * decay, 1, 0)
                key_back = key_back + decay * contract(chosen, query * decay, 0, 0)
            close = jnp.where(near, pairs, 0.0)
            query3, key3, cumul3 = tiles(query), tiles(keyrow), tiles(cumul)
            query_near = jnp.zeros_like(query3)
            key_near = jnp.zeros_like(key3)
            for step in range(TILE):
                column = jnp.sum(jnp.where(place == step, close, 0.0), axis=-1, keepdims=True)
                decay = jnp.exp(jnp.minimum(cumul3 - cumul3[:, step : step + 1], 0.0))
                weight = tiles(jnp.broadcast_to(column, (SPAN, DK))) * decay
                query_near = query_near + weight * key3[:, step : step + 1]
                total = jnp.sum(weight * query3, axis=1, keepdims=True)
                key_near = jnp.where(lane_row == step, total, key_near)
            query_back = query_back + query_near.reshape(SPAN, DK)
            key_back = key_back + key_near.reshape(SPAN, DK)
            query_back_ref[rows, narrow] = query_back.astype(jnp.bfloat16)
            key_back_ref[rows, narrow] = key_back.astype(jnp.bfloat16)
            cumul_back = query * query_back - keyrow * key_back
            ending = jnp.sum(after * carried, axis=0, keepdims=True)
            cumul_back = cumul_back + jnp.where(final, ending, 0.0)
            forget_back = exact(upper, cumul_back, 1, 0)
            logit_back_ref[rows, narrow] = forget_back * jax.nn.sigmoid(-logit_ref[rows, narrow]) / GATE_NORM
            carried = carried * jnp.exp(last) + contract(back, query * grown, 0, 0)
            after = before
    logit_back = logit_back_ref[...]
    lowrank_back_ref[...] = exact(logit_back, up_w[...].astype(jnp.float32), 1, 1).astype(jnp.bfloat16)
    expand_ref[...] = exact(lowrank_ref[...], logit_back, 0, 0)
    bias_ref[...] = jnp.sum(logit_back, axis=0, keepdims=True)


def call(kernel, outs, flops, scratch=()):
    whole = pl.BlockSpec(memory_space=pltpu.VMEM)

    def run(*args):
        moved = sum(a.size * a.dtype.itemsize for a in args)
        moved += sum(o.size * o.dtype.itemsize for o in outs)
        return pl.pallas_call(
            kernel,
            out_shape=tuple(outs),
            in_specs=[whole] * len(args),
            out_specs=tuple([whole] * len(outs)),
            scratch_shapes=list(scratch),
            compiler_params=pltpu.CompilerParams(vmem_limit_bytes=VMEM_LIMIT),
            cost_estimate=pl.CostEstimate(flops=flops, bytes_accessed=moved, transcendentals=0),
        )(*args)

    return run


def shape_of(rows, cols, kind=jnp.float32):
    return jax.ShapeDtypeStruct((rows, cols), kind)


def relay(own, total, axis, reverse):
    count = lax.axis_size(axis)
    pairs = [(i + 1, i) if reverse else (i, i + 1) for i in range(count - 1)]
    entering = None
    for _ in range(count - 1):
        sent = own if entering is None else own + total * entering
        entering = lax.ppermute(sent, axis, pairs)
    return jnp.zeros_like(own) if entering is None else entering


def split_halves(value, sent_ref, kept_ref, work_ref):
    half = value.shape[0] // 2
    work_ref[...] = value
    upper = upper_half()
    kept_ref[...] = work_ref[pl.ds(pl.multiple_of(upper * half, half), half), :]
    sent_ref[...] = work_ref[pl.ds(pl.multiple_of((1 - upper) * half, half), half), :]


def join_halves(kept_ref, other_ref, work_ref):
    half = kept_ref.shape[0]
    upper = upper_half()
    work_ref[pl.ds(pl.multiple_of(upper * half, half), half), :] = kept_ref[...]
    work_ref[pl.ds(pl.multiple_of((1 - upper) * half, half), half), :] = other_ref[...]
    return work_ref[...]


def gate_forward(local_ref, reach_ref, state_ref, outgate_ref, gain_ref, mixed_ref, gated_ref, sent_ref):
    heads = local_ref.shape[1] // DV
    for head in range(heads):
        narrow = slice(head * DK, (head + 1) * DK)
        wide = slice(head * DV, (head + 1) * DV)
        mixed = local_ref[:, wide] + contract(reach_ref[:, narrow], state_ref[wide, :], 1, 1)
        mixed_ref[:, wide] = mixed
        gate = outgate_ref[:, wide]
        gated = rms_apply(mixed, gain_ref[...]) * (gate * jax.nn.sigmoid(gate))
        gated_ref[:, wide] = gated.astype(jnp.bfloat16)
    sent_ref[...] = gated_ref[...].astype(jnp.float32)


def feed_forward(
    *refs,
    part,
):
    count = lax.axis_size("tensor")
    place = lax.axis_index("tensor")
    heads, output_w = refs[: 2 * count - 1], refs[2 * count - 1]
    size = heads[0].shape[0] // PARTS
    rows = slice(part * size, (part + 1) * size)
    span = heads[0].shape[1]
    attended = jnp.zeros((size, output_w.shape[1]), jnp.float32)
    for index, head_ref in enumerate(heads):
        step = (index + 1) // 2
        block = jnp.maximum(place - step, 0) if index % 2 else jnp.minimum(place + step, count - 1)
        weight = output_w[pl.ds(pl.multiple_of(block * span, span), span), :].astype(jnp.bfloat16)
        attended = attended + product(head_ref[rows, :].astype(jnp.bfloat16), weight)
    feed_forward_part(attended, rows, *refs[2 * count :])


def feed_forward_part(
    attended,
    rows,
    source_ref,
    upstream_ref,
    gain_ref,
    gate_w,
    up_w,
    down_w,
    middle_ref,
    second_ref,
    hidden_ref,
    back_ref,
    second_sent,
    second_kept,
    output_sent,
    output_kept,
    work_ref,
):
    units = gate_w.shape[0]
    middle = source_ref[rows, :].astype(jnp.float32) + attended
    middle_ref[...] = middle
    second = rms_apply(middle, gain_ref[...]).astype(jnp.bfloat16)
    second_ref[...] = second
    gate_pre = contract(second, gate_w[...], 1, 1, None)
    up_pre = contract(second, up_w[...], 1, 1, None)
    bell = jax.nn.sigmoid(gate_pre)
    silu = gate_pre * bell
    hidden = (silu * up_pre).astype(jnp.bfloat16)
    hidden_ref[...] = hidden
    hidden_back = contract(upstream_ref[rows, :], down_w[...], 1, 1, None)
    gate_back = (hidden_back * up_pre * (bell * (1.0 + gate_pre * (1.0 - bell)))).astype(jnp.bfloat16)
    up_back = (hidden_back * silu).astype(jnp.bfloat16)
    back_ref[:, :units] = gate_back
    back_ref[:, units:] = up_back
    terms = product(gate_back, gate_w[...]) + product(up_back, up_w[...])
    split_halves(terms, second_sent, second_kept, work_ref)
    split_halves(product(hidden, down_w[...]), output_sent, output_kept, work_ref)


def join_output(*refs):
    out_ref, work_ref = refs[-2:]
    size = out_ref.shape[0] // PARTS
    for part in range(PARTS):
        kept_ref, other_ref, middle_ref = refs[3 * part : 3 * part + 3]
        total = middle_ref[...] + join_halves(kept_ref, other_ref, work_ref)
        out_ref[part * size : (part + 1) * size, :] = total.astype(jnp.bfloat16)


def gate_backward(*refs):
    parts = refs[: 3 * PARTS]
    (
        upstream_ref,
        swiglu_gain_ref,
        weight_ref,
        mixed_ref,
        outgate_ref,
        gain_ref,
        reach_ref,
        middle_round_ref,
        middle_own_ref,
        mixed_back_ref,
        outgate_back_ref,
        group_ref,
        swiglu_ref,
        self_ref,
        work_ref,
        full_ref,
    ) = refs[3 * PARTS :]
    size = work_ref.shape[0]
    swiglu = jnp.zeros_like(swiglu_ref[...])
    for part in range(PARTS):
        kept_ref, other_ref, middle_ref = parts[3 * part : 3 * part + 3]
        rows = slice(part * size, (part + 1) * size)
        second_back = join_halves(kept_ref, other_ref, work_ref)
        middle = middle_ref[...]
        root = lax.rsqrt(jnp.mean(middle * middle, axis=-1, keepdims=True) + EPS)
        unit = middle * root
        swiglu = swiglu + jnp.sum(second_back * unit, axis=0, keepdims=True)
        inner = second_back * swiglu_gain_ref[...]
        back = root * (inner - unit * jnp.mean(inner * unit, axis=-1, keepdims=True))
        back = back + upstream_ref[rows, :].astype(jnp.float32)
        full_ref[rows, :] = back
        middle_round_ref[rows, :] = back.astype(jnp.bfloat16)
    swiglu_ref[...] = swiglu
    width = middle_own_ref.shape[1]
    middle_own_ref[...] = full_ref[:, pl.ds(pl.multiple_of(lax.axis_index("tensor") * width, width), width)]
    heads = mixed_ref.shape[1] // DV
    gated_back = contract(middle_round_ref[...], weight_ref[...], 1, 1, None)
    group = jnp.zeros((1, DV), jnp.float32)
    for head in range(heads):
        narrow = slice(head * DK, (head + 1) * DK)
        wide = slice(head * DV, (head + 1) * DV)
        mixed, gate, back = mixed_ref[:, wide], outgate_ref[:, wide], gated_back[:, wide]
        root = lax.rsqrt(jnp.mean(mixed * mixed, axis=-1, keepdims=True) + EPS)
        bell = jax.nn.sigmoid(gate)
        unit = mixed * root
        outer = back * (gate * bell)
        group = group + jnp.sum(outer * unit, axis=0, keepdims=True)
        outgate_back = back * unit * gain_ref[...] * (bell * (1.0 + gate * (1.0 - bell)))
        outgate_back_ref[:, wide] = outgate_back.astype(jnp.bfloat16)
        inner = outer * gain_ref[...]
        mixed_back = root * (inner - unit * jnp.mean(inner * unit, axis=-1, keepdims=True))
        mixed_back_ref[:, wide] = mixed_back
        self_ref[wide, :] = contract(mixed_back, reach_ref[:, narrow], 0, 0)
    group_ref[...] = group


def input_terms(
    source_ref,
    gain_ref,
    normed_ref,
    query_ref,
    key_ref,
    value_ref,
    outgate_ref,
    lowrank_ref,
    query_w,
    key_w,
    value_w,
    outgate_w,
    down_w,
    group_ref,
    swiglu_ref,
    expand_ref,
    bias_ref,
    small_ref,
    *rest,
):
    blocks, full_ref = rest[:-1], rest[-1]
    length, width = source_ref.shape
    terms = contract(query_ref[...], query_w[...], 1, 1, None)
    terms = terms + contract(key_ref[...], key_w[...], 1, 1, None)
    terms = terms + contract(value_ref[...], value_w[...], 1, 1, None)
    terms = terms + contract(outgate_ref[...], outgate_w[...], 1, 1, None)
    terms = terms + product(lowrank_ref[...], down_w[...])
    full_ref[...] = terms
    count = lax.axis_size("tensor")
    place = lax.axis_index("tensor")
    own = width // count

    def block(index):
        return full_ref[:, pl.ds(pl.multiple_of(index * own, own), own)]

    blocks[0][:length, :] = block(place)
    for step in range(1, count):
        blocks[2 * step - 1][:length, :] = block(jnp.minimum(count - step + place, count - 1))
        blocks[2 * step][:length, :] = block(jnp.maximum(place - count + step, 0))
    source = source_ref[...].astype(jnp.float32)
    root = lax.rsqrt(jnp.mean(source * source, axis=-1, keepdims=True) + EPS)
    along = terms * source
    rank = lowrank_ref.shape[1]
    small_ref[...] = jnp.zeros_like(small_ref)
    small_ref[:rank, :] = contract(lowrank_ref[...], normed_ref[...], 0, 0, None)
    small_ref[rank : rank + 1, :] = jnp.sum(along * root, axis=0, keepdims=True)
    small_ref[rank + 1 : rank + 2, :DV] = group_ref[...]
    inner = jnp.sum(along * gain_ref[...], axis=-1, keepdims=True)
    inner = jnp.broadcast_to(inner, (length, 128)).T[:1]
    for block_ref in blocks:
        block_ref[length:, :] = jnp.zeros((block_ref.shape[0] - length, own), jnp.float32)
        for line, start in enumerate(range(0, length, own)):
            end = min(start + own, length)
            block_ref[length + line : length + line + 1, : end - start] = inner[:, start:end]
    base = round_up(rank + 2, 8)
    small_ref[base : base + 1, :] = swiglu_ref[...]
    keys = bias_ref.shape[1]
    small_ref[base + 1 : base + 2, :keys] = bias_ref[...]
    many = width // keys
    for row in range(rank):
        start = row % many * keys
        line = base + 2 + row // many
        small_ref[line : line + 1, start : start + keys] = expand_ref[row : row + 1, :]


def gradient_terms(*refs):
    pairs, out_ref = refs[:-1], refs[-1]
    start = 0
    for left_ref, right_ref in zip(pairs[::2], pairs[1::2]):
        end = start + right_ref.shape[1]
        out_ref[:, start:end] = contract(left_ref[...], right_ref[...], 0, 0, None)
        start = end
    if start < out_ref.shape[1]:
        out_ref[:, start:] = jnp.zeros((out_ref.shape[0], out_ref.shape[1] - start), jnp.float32)


def round_up(count, multiple):
    return -(-count // multiple) * multiple


def gradients(pairs):
    columns = sum(right.shape[1] for _, right in pairs)
    width = pairs[0][0].shape[1]
    flat = [array for pair in pairs for array in pair]
    flops = 2 * width * columns * pairs[0][0].shape[0]
    (terms,) = call(gradient_terms, [shape_of(width, round_up(columns, 128))], flops)(*flat)
    return lax.psum_scatter(terms, ("dp", "seq"), scatter_dimension=0, tiled=True)


def gradient_blocks(*refs):
    pairs, outs = refs[:-4], refs[-4:]
    size = outs[0].shape[0] // len(ORDER)
    cut = outs[0].shape[1]
    place, own = lax.axis_index("dp"), lax.axis_index("seq")
    for far, (one_ref, two_ref) in ((1, outs[:2]), (0, outs[2:])):
        for index, step in enumerate(ORDER):
            block = (place ^ step) * 2 + (own ^ far)
            columns = pl.ds(pl.multiple_of(block * size, size), size)
            rows = slice(index * size, (index + 1) * size)
            start = 0
            for left_ref, right_ref in zip(pairs[::2], pairs[1::2]):
                count = right_ref.shape[1]
                block_sum = contract(left_ref[:, columns], right_ref[...], 0, 0, None)
                here = min(max(cut - start, 0), count)
                if here > 0:
                    one_ref[rows, start : start + here] = block_sum[:, :here]
                if here < count:
                    two_ref[rows, start + here - cut : start + count - cut] = block_sum[:, here:]
                start += count
            if start < cut + two_ref.shape[1]:
                two_ref[rows, start - cut :] = jnp.zeros((size, cut + two_ref.shape[1] - start), jnp.float32)


def gradient_start(pairs):
    columns = sum(right.shape[1] for _, right in pairs)
    width = pairs[0][0].shape[1]
    if direct():
        flat = [array for pair in pairs for array in pair]
        columns = round_up(columns, 128)
        cut = columns // 256 * 128
        halves = [shape_of(width // 2, cut), shape_of(width // 2, columns - cut)]
        flops = 2 * width * columns * pairs[0][0].shape[0]
        outs = call(gradient_blocks, halves * 2, flops)(*flat)
        return scatter_start(outs[:2], outs[2:])
    whole = jnp.concatenate([product(left.T, right) for left, right in pairs], axis=1)
    return lax.psum_scatter(whole, ("dp", "seq"), scatter_dimension=0, tiled=True)


def gradient_end(begun):
    return jnp.concatenate(scatter_end(*begun), axis=1) if direct() else begun


def on_device(
    block_input,
    mixer_gain,
    query_weight,
    key_weight,
    value_weight,
    outgate_weight,
    decay_down,
    decay_up,
    decay_bias,
    group_gain,
    output_weight,
    swiglu_gain,
    gate_weight,
    up_weight,
    down_weight,
    cotangent,
):
    rounded = jnp.bfloat16
    source, upstream = block_input[0], cotangent[0]
    length, width = source.shape
    keys, values, units = query_weight.shape[1], value_weight.shape[1], gate_weight.shape[1]
    heads = keys // DK
    rank = decay_down.shape[1]
    size = length // PARTS
    half = shape_of(size // 2, width)
    work = pltpu.VMEM((size, width), jnp.float32)
    state = {}
    share = values // (lax.axis_size("dp") * lax.axis_size("seq"))
    place = lax.axis_index("dp") * lax.axis_size("seq") + lax.axis_index("seq")
    share_rows = lax.dynamic_slice_in_dim(output_weight, place * share, share, 0).astype(jnp.float32)
    full_output_weight = lax.all_gather(share_rows, ("tensor", "dp", "seq"), axis=0, tiled=True)
    (
        normed,
        query,
        keyrow,
        value,
        outgate,
        lowrank,
        logit,
        cumul,
        reach,
        local,
        local_state,
        decay_total,
    ) = call(
        mix_forward,
        [
            shape_of(length, width, rounded),
            shape_of(length, keys),
            shape_of(length, keys),
            shape_of(length, values),
            shape_of(length, values),
            shape_of(length, rank),
            shape_of(length, keys),
            shape_of(length, keys),
            shape_of(length, keys),
            shape_of(length, values),
            shape_of(values, DK),
            shape_of(heads, DK),
        ],
        2 * length * width * (2 * keys + 2 * values),
    )(
        source,
        mixer_gain[None],
        query_weight,
        key_weight,
        value_weight,
        outgate_weight,
        decay_down.T,
        decay_up,
        decay_bias[None],
    )
    decay_rows = jnp.repeat(decay_total, DV, axis=0)
    incoming = relay(local_state, decay_rows, "seq", False)
    mixed, gated, sent = call(
        gate_forward,
        [shape_of(length, values), shape_of(length, values, rounded), shape_of(length, values)],
        20 * length * values,
    )(local, reach, incoming, outgate, group_gain[None])
    heads_out = line_gather(sent)
    parts = []
    for part in range(PARTS):
        parts.append(
            call(
                functools.partial(feed_forward, part=part),
                [
                    shape_of(size, width),
                    shape_of(size, width, rounded),
                    shape_of(size, units, rounded),
                    shape_of(size, 2 * units, rounded),
                    half,
                    half,
                    half,
                    half,
                ],
                12 * size * width * units,
                scratch=[work],
            )(*heads_out, full_output_weight, source, upstream, swiglu_gain[None], gate_weight.T, up_weight.T, down_weight)
        )
    second_sums = []
    for part in parts:
        second_sums += [*halves_sum(part[4], part[5], state), part[0]]
    second = jnp.concatenate([part[1] for part in parts], axis=0)
    hidden = jnp.concatenate([part[2] for part in parts], axis=0)
    units_back = jnp.concatenate([part[3] for part in parts], axis=0)
    wide_total = gradients([(second, units_back), (upstream, hidden)])
    output_sums = []
    for part in parts:
        output_sums += [*halves_sum(part[6], part[7], state), part[0]]
    (block_output,) = call(
        join_output, [shape_of(length, width, rounded)], length * width, scratch=[work]
    )(*output_sums)
    count = lax.axis_size("tensor")
    own = width // count
    middle_round, middle_own, mixed_back, outgate_round, group_part, swiglu_part, self_gradient = call(
        gate_backward,
        [
            shape_of(length, width, rounded),
            shape_of(length, own),
            shape_of(length, values),
            shape_of(length, values, rounded),
            shape_of(1, DV),
            shape_of(1, width),
            shape_of(values, DK),
        ],
        2 * length * width * values,
        scratch=[work, pltpu.VMEM((length, width), jnp.float32)],
    )(*second_sums, upstream, swiglu_gain[None], output_weight, mixed, outgate, group_gain[None], reach)
    outgoing = relay(self_gradient, decay_rows, "seq", True)
    query_round, key_round, value_round, lowrank_round, expand_part, bias_part = call(
        mix_backward,
        [
            shape_of(length, keys, rounded),
            shape_of(length, keys, rounded),
            shape_of(length, values, rounded),
            shape_of(length, rank, rounded),
            shape_of(rank, keys),
            shape_of(1, keys),
        ],
        20 * length * DK * values,
        scratch=[
            pltpu.VMEM((length // SPAN, DV, DK), jnp.float32),
            pltpu.VMEM((length, keys), jnp.float32),
        ],
    )(query, keyrow, value, cumul, logit, lowrank, mixed_back, incoming, outgoing, decay_up)
    many = width // keys
    split_rows = round_up(2 + round_up(rank, many) // many, 8)
    shared_rows = round_up(rank + 2, 8)
    lines = -(-length // own)
    small, own_terms, *steps = call(
        input_terms,
        [shape_of(shared_rows + split_rows, width)]
        + [shape_of(length + round_up(lines, 8), own)] * (2 * count - 1),
        2 * length * width * (2 * keys + 2 * values),
        scratch=[pltpu.VMEM((length, width), jnp.float32)],
    )(
        source,
        mixer_gain[None],
        normed,
        query_round,
        key_round,
        value_round,
        outgate_round,
        lowrank_round,
        query_weight,
        key_weight,
        value_weight,
        outgate_weight,
        decay_down.T,
        group_part,
        swiglu_part,
        expand_part,
        bias_part,
    )
    right = left = None
    for step in range(1, count):
        sent = steps[2 * step - 2] if right is None else steps[2 * step - 2] + right
        right = lax.ppermute(sent, "tensor", [(i, i + 1) for i in range(step)])
        sent = steps[2 * step - 1] if left is None else steps[2 * step - 1] + left
        left = lax.ppermute(sent, "tensor", [(count - 1 - i, count - 2 - i) for i in range(step)])
    mixer_begun = gradient_start(
        [
            (normed, query_round),
            (normed, key_round),
            (normed, value_round),
            (normed, outgate_round),
            (middle_round, gated),
        ],
    )
    mixer_total = gradient_end(mixer_begun)
    small = butterfly(small, "seq")
    small = butterfly(small, "dp")
    shared, mask = small[:shared_rows], 1
    while mask < count:
        shared = shared + flip(shared, "tensor", mask)
        mask *= 2
    place = lax.axis_index("tensor")
    total = own_terms if right is None else own_terms + right + left
    normed_back = total[:length]
    inner = total[length : length + lines].reshape(-1, 1)[:length]
    wide_source = source.astype(jnp.float32)
    root = lax.rsqrt(jnp.mean(wide_source * wide_source, axis=-1, keepdims=True) + EPS)
    source_own = column_block(wide_source, place, own)
    weighted = normed_back * lax.dynamic_slice_in_dim(mixer_gain, place * own, own, 0)
    source_back = root * weighted - source_own * (root * root * root * inner / width)
    mixer_part = lax.dynamic_slice_in_dim(shared[rank], place * own, own, 0)
    ends = (keys, 2 * keys, 2 * keys + values, 2 * keys + 2 * values)
    expand_rows = small[shared_rows + 2 : shared_rows + 2 + round_up(rank, many) // many]
    return (
        block_output[None],
        (middle_own + source_back)[None],
        mixer_part,
        mixer_total[:, : ends[0]],
        mixer_total[:, ends[0] : ends[1]],
        mixer_total[:, ends[1] : ends[2]],
        mixer_total[:, ends[2] : ends[3]],
        shared[:rank].T,
        expand_rows.reshape(-1, keys)[:rank],
        small[shared_rows + 1, :keys],
        shared[rank + 1, :DV],
        mixer_total[:, ends[3] :].T,
        small[shared_rows],
        wide_total[:, :units],
        wide_total[:, units : 2 * units],
        wide_total[:, 2 * units : 3 * units].T,
    )


def solution(mesh):
    in_specs = (
        P("dp", "seq", None),
        P(),
        P(None, "tensor"),
        P(None, "tensor"),
        P(None, "tensor"),
        P(None, "tensor"),
        P(),
        P(None, "tensor"),
        P("tensor"),
        P(),
        P("tensor", None),
        P(),
        P(None, "tensor"),
        P(None, "tensor"),
        P("tensor", None),
        P("dp", "seq", None),
    )
    out_specs = (
        P("dp", "seq", None),
        P("dp", "seq", "tensor"),
        P("tensor"),
        P(("dp", "seq"), "tensor"),
        P(("dp", "seq"), "tensor"),
        P(("dp", "seq"), "tensor"),
        P(("dp", "seq"), "tensor"),
        P(),
        P(None, "tensor"),
        P("tensor"),
        P(),
        P("tensor", ("dp", "seq")),
        P(),
        P(("dp", "seq"), "tensor"),
        P(("dp", "seq"), "tensor"),
        P("tensor", ("dp", "seq")),
    )
    return jax.shard_map(on_device, mesh=mesh, in_specs=in_specs, out_specs=out_specs, check_vma=False)
```
